32 devices in a mesh: gx: 8 (over z, x), gy: 4 (over y, core).
Axes of the slice: x: 2, y: 2, z: 4, core: 2. Of those that a mesh axis runs over, the one named last changes fastest.
Arguments:
- shape_coef: float32 [8, 4, 16, 6, 169], P('gx', 'gy'), may hold values from -6 to 6
- cotangent: float32 [8, 4, 16, 3, 625], P('gx', 'gy'), may hold values from -6 to 6
- neighbours: int32 [8, 4, 16, 12], P('gx', 'gy'), may hold values from 0 to 511, as said below
- counts: int32 [8, 4, 16], P('gx', 'gy'), may hold values from 1 to 12, as said below
- synth: float32 [625, 169], replicated, may hold values from -0.5 to 0.5
- weights: float32 [625], replicated, may hold values from 0.4 to 1.6
- stiffness: float32 [169], replicated, may hold values from 0.3 to 3
Outputs:
- coef_grad: float32 [8, 4, 16, 3, 169], P('gx', 'gy')
The draws below stay inside these ranges and needn't reach their ends.
Inputs may be any that keep to these rules, and one draw needn't show every extreme that they name: `neighbours`: slot 0 of every capsule names the capsule itself; every other slot names a capsule held by the same device or by one of the eight devices beside it along gx and gy, taken periodically. `counts`: every device has a capsule with all 12 slots live.
All inputs are finite; a program needn't handle non-finite values.
Results may differ from the reference program's by a relative error of at most 0.0003.
Values sent between devices are 32-bit elements; how exact they have to be, the bound alone decides.
No kernel may reach another device: no remote copies, remote signals or barrier semaphores. Data moves between devices by JAX's collectives and lax.ppermute only.
A program may use at most 64 MiB of HBM per device.

```python
import math
import jax
import jax.numpy as jnp
from jax import lax

NSH = 169
NPTS = 625
NB = 12
CAPS_DEV = 16
N_GX = 8
N_GY = 4


def draw_neighbours(key, part):
    array_shape = (N_GX, N_GY, CAPS_DEV, NB)
    key_x, key_y, key_c = jax.random.split(jax.random.fold_in(key, 11), 3)
    step_x = jax.random.randint(key_x, array_shape, -1, 2)
    step_y = jax.random.randint(key_y, array_shape, -1, 2)
    local = jax.random.randint(key_c, array_shape, 0, CAPS_DEV)
    grid_x = lax.broadcasted_iota(jnp.int32, array_shape, 0)
    grid_y = lax.broadcasted_iota(jnp.int32, array_shape, 1)
    capsule = lax.broadcasted_iota(jnp.int32, array_shape, 2)
    slot = lax.broadcasted_iota(jnp.int32, array_shape, 3)
    near_x = (grid_x + step_x + N_GX) % N_GX
    near_y = (grid_y + step_y + N_GY) % N_GY
    others = (near_x * N_GY + near_y) * CAPS_DEV + local
    itself = (grid_x * N_GY + grid_y) * CAPS_DEV + capsule
    return jnp.where(slot == 0, itself, others).astype(jnp.int32)


def draw_counts(key, part):
    array_shape = (N_GX, N_GY, CAPS_DEV)
    key_a, key_b = jax.random.split(jax.random.fold_in(key, 23))
    drawn = jax.random.randint(key_a, array_shape, 1, NB + 1)
    chosen = jax.random.randint(key_b, (N_GX, N_GY, 1), 0, CAPS_DEV)
    capsule = lax.broadcasted_iota(jnp.int32, array_shape, 2)
    return jnp.where(capsule == chosen, NB, drawn).astype(jnp.int32)


def levels(key, shape, shards, low, high):
    def one(dim, shards_of):
        steps = jax.random.uniform(jax.random.fold_in(jax.random.fold_in(key, 6), dim), (shards_of,), jnp.float32, low / len(shards), high / len(shards))
        return jnp.repeat(jnp.exp(steps), shape[dim] // shards_of).reshape((-1,) + (1,) * (len(shape) - dim - 1))

    loudness = one(*shards[0])
    for cut in shards[1:]:
        loudness = loudness * one(*cut)
    return loudness


def noise(key, dims, spread, limit, cuts=(), held_as=jnp.bfloat16):
    gain = levels(key, dims, cuts, -0.22, 0.18) if cuts else 1.0
    values = jax.random.normal(key, dims, jnp.float32) * spread * gain
    return jnp.minimum(jnp.maximum(values, -limit), limit).astype(held_as)


def setup_inputs(seed: int = 0) -> dict:
    keys = jax.random.split(jax.random.key(seed), 8)
    shape_coef = noise(keys[0], (N_GX, N_GY, CAPS_DEV, 6, NSH), 1.0, 6.0, ((0, 8), (1, 4)), jnp.float32)
    cotangent = noise(keys[1], (N_GX, N_GY, CAPS_DEV, 3, NPTS), 1.0, 6.0, ((0, 8), (1, 4)), jnp.float32)
    neighbours = draw_neighbours(jax.random.fold_in(keys[7], 71), 0)
    counts = draw_counts(jax.random.fold_in(keys[7], 71), 0)
    synth = noise(keys[4], (NPTS, NSH), NSH ** -0.5, 0.5, (), jnp.float32)
    weights = jnp.clip(jax.random.uniform(keys[5], (NPTS,), jnp.float32, 0.4, 1.6), 0.4, 1.6)
    stiffness = jnp.clip(jnp.exp(jax.random.uniform(keys[6], (NSH,), jnp.float32, math.log(0.3), math.log(3.0))), 0.3, 3.0)
    return dict(shape_coef=shape_coef, cotangent=cotangent, neighbours=neighbours, counts=counts, synth=synth, weights=weights, stiffness=stiffness)


DELTA_SQ = 0.0625

def upsample(coefs, synth):
    return jnp.einsum('ckp,ip->cki', coefs, synth, precision=lax.Precision.HIGHEST)

def pair_kernel(target_point, source, normal):
    numer = jnp.zeros((target_point.shape[1], source.shape[1]), jnp.float32)
    base = jnp.zeros((target_point.shape[1], source.shape[1]), jnp.float32) + DELTA_SQ
    for comp in range(3):
        differ = target_point[comp][:, None] - source[comp][None, :]
        base = base + differ * differ
        numer = numer + differ * normal[comp][None, :]
    return numer / (base * jnp.sqrt(base))

def reference(shape_coef, cotangent, neighbours, counts, synth, weights, stiffness):
    total = shape_coef.shape[0] * shape_coef.shape[1] * shape_coef.shape[2]
    points = upsample(shape_coef.reshape(total, 6, NSH), synth)
    cot_all = cotangent.reshape(total, 3, NPTS)
    capsule_index = neighbours.reshape(total, NB).astype(jnp.int32)
    live_count = counts.reshape(total).astype(jnp.int32)

    def visit_entry(target_point, accumulated_sum):
        tpts = points[target_point, 0:3]
        for slot in range(NB):
            source = capsule_index[target_point, slot]
            spts = points[source]
            kernel = pair_kernel(tpts, spts[0:3], spts[3:6])
            term = jnp.dot(cot_all[target_point], kernel, precision=lax.Precision.HIGHEST) * weights[None, :]
            live = (slot < live_count[target_point]).astype(jnp.float32)
            accumulated_sum = accumulated_sum.at[source].add(term * live)
        return accumulated_sum
    source_grad = lax.fori_loop(0, total, visit_entry, jnp.zeros((total, 3, NPTS), jnp.float32))
    grad = jnp.einsum('cki,ip->ckp', source_grad, synth, precision=lax.Precision.HIGHEST) * stiffness[None, None, :]
    return grad.reshape(shape_coef.shape[0], shape_coef.shape[1], shape_coef.shape[2], 3, NSH)
```

```python
import functools

import jax
import jax.numpy as jnp
from jax import lax
from jax.experimental import pallas as pl
from jax.experimental.pallas import tpu as pltpu
from jax.sharding import PartitionSpec as P


F32, BF16 = jnp.float32, jnp.bfloat16
DELTA_SQ = 0.0625
RADIUS_SQ_MAX = 64.0
HIGHEST = lax.Precision.HIGHEST
LANES = 128
ROWS = 8
TILE = 256
LEAD = 2
VMEM = pl.BlockSpec(memory_space=pltpu.VMEM)
SMEM = pl.BlockSpec(memory_space=pltpu.SMEM)


def up(n, m):
    return -(-n // m) * m


def shifted(block, axis, distance):
    devices = range(lax.axis_size(axis))
    route = [((i - distance) % len(devices), i) for i in devices]
    return lax.ppermute(block, axis, route)


def split3(v):
    high = v.astype(BF16)
    rest = v - high.astype(F32)
    mid = rest.astype(BF16)
    return high, mid, (rest - mid.astype(F32)).astype(BF16)


def cat(*xs):
    return jnp.concatenate(xs, axis=0)


def square(p):
    return p[0:1] * p[0:1] + p[1:2] * p[1:2] + p[2:3] * p[2:3]


def target_factor(p):
    row = lax.broadcasted_iota(jnp.int32, p.shape, 0)
    tail = jnp.where(row == 4, square(p) + DELTA_SQ, 0.0)
    return jnp.where(row < 3, p, jnp.where(row == 3, 1.0, tail))


def source_factor(p):
    row = lax.broadcasted_iota(jnp.int32, p.shape, 0)
    tail = jnp.where(row == 4, 1.0, 0.0)
    return jnp.where(row < 3, -2.0 * p, jnp.where(row == 3, square(p), tail))


def prepare_kernel(code_ref, coef_ref, cot_ref, basis_ref, list_ref, count_ref, points_ref, factor_ref, rows_ref):
    caps, _, npts = cot_ref.shape
    nlist, length = list_ref.shape
    flat = coef_ref[...].reshape(caps * ROWS, coef_ref.shape[2])
    points = jnp.dot(flat, basis_ref[...], precision=HIGHEST, preferred_element_type=F32)
    points_ref[...] = points.reshape(caps, ROWS, npts)

    def each_target(t, _):
        p = points_ref[t]
        w1, w2, w3 = [w.astype(F32) for w in split3(target_factor(p))]
        pad = jnp.zeros((LANES - 6 * ROWS, npts), F32)
        factor_ref[t] = cat(w1, w1, w2, w2, w1, w3, pad).T.astype(BF16)
        c = cot_ref[t]
        c3 = c[0:3]
        a = cat(c3 * p[0:1], c3 * p[1:2], c3 * p[2:3], c3, jnp.zeros((4, npts), F32))
        rows_ref[t] = cat(*split3(a))
        return 0

    lax.fori_loop(0, caps, each_target, 0)
    for c in range(nlist):
        count_ref[c] = LEAD

    def each_entry(e, _):
        code = code_ref[e]
        c = code >> 16
        n = count_ref[c]
        list_ref[c, n] = code & 65535
        count_ref[c] = n + 1
        return 0

    lax.fori_loop(0, code_ref.shape[0], each_entry, 0)


def prepare(code, coef, cot, basis, nlist):
    caps, _, npts = cot.shape
    length = up(code.shape[0] + 2 * LEAD, LANES)
    return pl.pallas_call(
        prepare_kernel,
        out_shape=(
            jax.ShapeDtypeStruct((nlist, length), jnp.int32),
            jax.ShapeDtypeStruct((nlist,), jnp.int32),
            jax.ShapeDtypeStruct((caps, ROWS, npts), F32),
            jax.ShapeDtypeStruct((caps, npts, LANES), BF16),
            jax.ShapeDtypeStruct((caps, 6 * ROWS, npts), BF16),
        ),
        in_specs=[SMEM, VMEM, VMEM, VMEM],
        out_specs=(SMEM, SMEM, VMEM, VMEM, VMEM),
        name="prepare",
    )(code, coef, cot, basis)


def pairs_kernel(which, nsrc, list_ref, count_ref, target_ref, factor_ref, rows_ref, cot_ref, basis_ref, synth_ref, weight_ref, *rest):
    coef_refs, out_refs = rest[:nsrc], rest[nsrc : 2 * nsrc]
    points, total, base_sc, high_sc, low_sc, column, entries = rest[2 * nsrc :]
    caps, _, npts = target_ref.shape
    dummy = points.shape[0] - 1
    tiles = [(j, min(TILE, npts - j)) for j in range(0, npts, TILE)]
    total[...] = jnp.zeros_like(total)
    points[dummy] = jnp.zeros((ROWS, npts), F32)
    at = 0
    spread = jnp.max(functools.reduce(jnp.maximum, [square(target_ref[t]) for t in range(caps)]))
    for coef_ref in coef_refs:
        held = coef_ref.shape[0]
        for c in range(0, held, caps):
            flat = coef_ref[c : c + caps].reshape(caps * ROWS, coef_ref.shape[2])
            block = jnp.dot(flat, basis_ref[...], precision=HIGHEST, preferred_element_type=F32)
            block = block.reshape(caps, ROWS, npts)
            points[at : at + caps] = block
            sizes = [square(block[t]) for t in range(caps)]
            spread = jnp.maximum(spread, jnp.max(functools.reduce(jnp.maximum, sizes)))
            at += caps

    count = count_ref[which]
    live = count - LEAD

    def copy_entry(k, _):
        inside = jnp.logical_and(k >= LEAD, k < count)
        entries[k] = jnp.where(inside, list_ref[which, k], dummy)
        return 0

    lax.fori_loop(0, count + LEAD, copy_entry, 0)

    def entry(k):
        code = entries[k]
        return code >> 10, code & 1023

    def add_term(s, j, jc, sums):
        y = points[s, :, j : j + jc]
        plain = sums[9:12]
        term = y[3:4] * (sums[0:3] - y[0:1] * plain)
        term += y[4:5] * (sums[3:6] - y[1:2] * plain)
        term += y[5:6] * (sums[6:9] - y[2:3] * plain)
        total[s, 0:3, j : j + jc] += term

    def fast_step(k, _):
        t, s = entry(k)
        t_next, s_next = entry(k + LEAD)
        u1, u2, u3 = [u.astype(F32) for u in split3(source_factor(points[s_next]))]
        pad = jnp.zeros((LANES - 6 * ROWS, npts), F32)
        source = cat(u1, u2, u1, u2, u3, u1, pad).astype(BF16)
        for j, jc in tiles:
            d1 = jnp.dot(rows_ref[t], high_sc[:, j : j + jc], preferred_element_type=F32)
            d2 = jnp.dot(rows_ref[t, 0:32], low_sc[:, j : j + jc], preferred_element_type=F32)
            add_term(s, j, jc, d1[0:16] + d1[16:32] + d1[32:48] + d2[0:16] + d2[16:32])
            r = lax.rsqrt(base_sc[:, j : j + jc])
            r3 = r * r * r
            high = r3.astype(BF16)
            high_sc[:, j : j + jc] = high
            low_sc[:, j : j + jc] = (r3 - high.astype(F32)).astype(BF16)
            base_sc[:, j : j + jc] = jnp.dot(
                factor_ref[t_next], source[:, j : j + jc], preferred_element_type=F32
            )
        return 0

    def exact_step(k, _):
        t, s = entry(k)
        pad = jnp.zeros((LANES - ROWS, npts), F32)
        column[...] = cat(target_ref[t], pad).T
        y = points[s]

        def each_chunk(i, acc):
            start = pl.multiple_of(i * LANES, LANES)
            x = column[pl.ds(start, LANES), :]
            numer, base = 0.0, DELTA_SQ
            for d in range(3):
                differ = x[:, d : d + 1] - y[d : d + 1]
                base = base + differ * differ
                numer = numer + differ * y[3 + d : 4 + d]
            kernel = numer / (base * jnp.sqrt(base))
            cot = cot_ref[t, :, pl.ds(start, LANES)]
            return acc + jnp.dot(cot, kernel, precision=HIGHEST, preferred_element_type=F32)

        term = lax.fori_loop(0, npts // LANES, each_chunk, jnp.zeros((ROWS, npts), F32))
        total[s] += term
        return 0

    expands = spread <= RADIUS_SQ_MAX

    @pl.when(jnp.logical_and(expands, live > 0))
    def _():
        lax.fori_loop(0, count, fast_step, 0)

    @pl.when(jnp.logical_not(expands))
    def _():
        lax.fori_loop(LEAD, count, exact_step, 0)

    at = 0
    for coef_ref, out_ref in zip(coef_refs, out_refs):
        held = coef_ref.shape[0]
        scaled = total[at : at + held] * weight_ref[...][None]
        flat = scaled.reshape(held * ROWS, npts)
        grad = jnp.dot(flat, synth_ref[...], precision=HIGHEST, preferred_element_type=F32)
        grad = grad.reshape(held, ROWS, grad.shape[1])
        for d in range(3):
            out_ref[d] = grad[:, d]
        at += held


def pairs(which, name, shared, coefs):
    lists, counts, points, factor, rows, cot, basis, synth, weights = shared
    npts, width = synth.shape
    nsources = sum(c.shape[0] for c in coefs)
    held = lists.shape[1]
    flops = 2 * 4 * nsources * npts * npts * 64
    return pl.pallas_call(
        functools.partial(pairs_kernel, which, len(coefs)),
        out_shape=tuple(jax.ShapeDtypeStruct((3, c.shape[0], width), F32) for c in coefs),
        in_specs=[SMEM, SMEM] + [VMEM] * (7 + len(coefs)),
        out_specs=tuple(VMEM for _ in coefs),
        scratch_shapes=[
            pltpu.VMEM((nsources + 1, ROWS, npts), F32),
            pltpu.VMEM((nsources + 1, ROWS, npts), F32),
            pltpu.VMEM((npts, npts), F32),
            pltpu.VMEM((npts, npts), BF16),
            pltpu.VMEM((npts, npts), BF16),
            pltpu.VMEM((npts, LANES), F32),
            pltpu.SMEM((held + 2 * LEAD,), jnp.int32),
        ],
        cost_estimate=pl.CostEstimate(flops=flops, bytes_accessed=1 << 22, transcendentals=0),
        name=name,
    )(lists, counts, points, factor, rows, cot, basis, synth, weights, *coefs)


def shards(shape_coef, cotangent, neighbours, counts, synth, weights, stiffness):
    caps, nrows, nsh = shape_coef.shape[2:]
    npoints = synth.shape[0]
    slots = neighbours.shape[3]
    width_x, width_y = lax.axis_size("gx"), lax.axis_size("gy")
    here_x, here_y = lax.axis_index("gx"), lax.axis_index("gy")
    npts, wide = up(npoints, LANES), up(nsh, TILE)

    coef = jnp.pad(shape_coef.reshape(caps, nrows, nsh), ((0, 0), (0, ROWS - nrows), (0, wide - nsh)))
    from_below = shifted(coef, "gy", 1)
    from_above = shifted(coef, "gy", -1)
    column = jnp.concatenate([from_below, coef, from_above])
    from_left = shifted(column, "gx", 1)
    from_right = shifted(column, "gx", -1)

    index = neighbours.reshape(caps, slots)
    off_x = (index // (width_y * caps) - here_x + 1 + width_x) % width_x
    off_y = (index // caps % width_y - here_y + 1 + width_y) % width_y
    cap = index % caps
    target = lax.broadcasted_iota(jnp.int32, (caps, slots), 0)
    live = lax.broadcasted_iota(jnp.int32, (caps, slots), 1) < counts.reshape(caps, 1)
    local = off_y == 1
    side = jnp.where(off_x == 2, 3 * caps, 0) + off_y * caps + cap
    near = jnp.where(local, cap, jnp.where(off_y == 2, caps, 0) + cap)
    source = jnp.where(off_x == 1, near, side)
    group = jnp.where(off_x == 1, jnp.where(local, 0, 1), 2)
    group = jnp.where(live, group, 3)
    code = ((group << 16) + (target << 10) + source).reshape(-1)

    cot = jnp.pad(cotangent.reshape(caps, 3, npoints), ((0, 0), (0, ROWS - 3), (0, npts - npoints)))
    synth_pad = jnp.pad(synth, ((0, npts - npoints), (0, wide - nsh)))
    basis = jnp.pad(synth.T, ((0, wide - nsh), (0, npts - npoints)))
    weight_pad = jnp.pad(weights, (0, npts - npoints)).reshape(1, npts)

    prepared = prepare(code, coef, cot, basis, 4)
    shared = (*prepared, cot, basis, synth_pad, weight_pad)
    (mine,) = pairs(0, "pairs_local", shared, [coef])
    to_left, to_right = pairs(2, "pairs_gx", shared, [from_left, from_right])
    below_right = shifted(to_left, "gx", -1)
    above_left = shifted(to_right, "gx", 1)
    to_below, to_above = pairs(1, "pairs_gy", shared, [from_below, from_above])
    crossed = (below_right + above_left).reshape(3, 3, caps, wide)
    to_below = to_below + crossed[:, 0]
    to_above = to_above + crossed[:, 2]
    back = shifted(to_below, "gy", -1) + shifted(to_above, "gy", 1)
    grad = mine + crossed[:, 1] + back
    grad = grad[:, :, :nsh] * stiffness
    return grad.transpose(1, 0, 2).reshape(1, 1, caps, 3, nsh)


def solution(mesh):
    placed = (
        P("gx", "gy", None, None, None),
        P("gx", "gy", None, None, None),
        P("gx", "gy", None, None),
        P("gx", "gy", None),
        P(),
        P(),
        P(),
    )
    return jax.shard_map(
        shards,
        mesh=mesh,
        in_specs=placed,
        out_specs=P("gx", "gy", None, None, None),
        check_vma=False,
    )
```

```python
import functools

import jax
import jax.numpy as jnp
from jax import lax
from jax.experimental import pallas as pl
from jax.experimental.pallas import tpu as pltpu
from jax.sharding import PartitionSpec as P


F32, BF16 = jnp.float32, jnp.bfloat16
DELTA_SQ = 0.0625
RADIUS_SQ_MAX = 64.0
HIGHEST = lax.Precision.HIGHEST
LANES = 128
ROWS = 8
VMEM_LIMIT = 28 << 20
TILE = 256
UNROLL = 2
VMEM = pl.BlockSpec(memory_space=pltpu.VMEM)
SMEM = pl.BlockSpec(memory_space=pltpu.SMEM)
ANY = pl.BlockSpec(memory_space=pl.ANY)


def up(n, m):
    return -(-n // m) * m


def shifted(block, axis, distance):
    devices = range(lax.axis_size(axis))
    route = [((i - distance) % len(devices), i) for i in devices]
    return lax.ppermute(block, axis, route)


def moved(block, dx, dy):
    wx, wy = lax.axis_size("gx"), lax.axis_size("gy")
    grid = [(x, y) for x in range(wx) for y in range(wy)]
    route = [(x * wy + y, (x + dx) % wx * wy + (y + dy) % wy) for x, y in grid]
    return lax.ppermute(block, ("gx", "gy"), route)


def put(ref, value):
    for lane in range(ref.shape[0]):
        ref[lane, 0 : value.shape[0]] = value[:, lane * LANES : (lane + 1) * LANES]


def take(ref, at, stride):
    parts = [ref[lane, pl.ds(at, ROWS, stride=stride), :] for lane in range(ref.shape[0])]
    return jnp.concatenate(parts, axis=1)


def farthest(rows, caps, nblocks):
    sizes = []
    for start in range(0, rows.shape[0], rows.shape[0] // nblocks):
        x, y, z = [rows[at : at + caps] for at in range(start, start + 3 * caps, caps)]
        sizes.append(x * x + y * y + z * z)
    return jnp.max(functools.reduce(jnp.maximum, sizes))


def quotient(v, n):
    return v >> (n.bit_length() - 1) if n & (n - 1) == 0 else lax.div(v, jnp.int32(n))


def offset(block, here, width):
    step = block - here + 1
    return jnp.where(step < 0, step + width, jnp.where(step >= width, step - width, step))


def split3(v):
    high = v.astype(BF16)
    rest = v - high.astype(F32)
    mid = rest.astype(BF16)
    return high, mid, (rest - mid.astype(F32)).astype(BF16)


def cat(*xs):
    return jnp.concatenate(xs, axis=0)


def square(p):
    return p[0:1] * p[0:1] + p[1:2] * p[1:2] + p[2:3] * p[2:3]


def target_factor(p):
    row = lax.broadcasted_iota(jnp.int32, p.shape, 0)
    tail = jnp.where(row == 4, square(p) + DELTA_SQ, 0.0)
    return jnp.where(row < 3, p, jnp.where(row == 3, 1.0, tail))


def source_factor(p):
    row = lax.broadcasted_iota(jnp.int32, p.shape, 0)
    tail = jnp.where(row == 4, 1.0, 0.0)
    return jnp.where(row < 3, -2.0 * p, jnp.where(row == 3, square(p), tail))


def prepare_kernel(
    where_ref, near_ref, live_ref, coef_ref, cot_ref, synth_ref,
    list_ref, count_ref, reach_ref, target_ref, factor_ref, rows_ref, cotan_ref, basis_ref,
    code_v, code_s, points, cots, sem, *, width_x, width_y,
):
    slots, caps = near_ref.shape
    nsh, npoints = synth_ref.shape
    npts = basis_ref.shape[1]
    nrows = coef_ref.shape[0] // caps

    index = near_ref[...]
    column = quotient(index, caps)
    line = quotient(column, width_y)
    cap = index - column * caps
    off_x = offset(line, where_ref[0], width_x)
    off_y = offset(column - line * width_y, where_ref[1], width_y)
    block_x = jnp.where(off_x == 2, 3, 0) + off_y
    block_y = jnp.where(off_y == 2, 1, 0)
    centre = off_x == 1
    block = jnp.where(centre, block_y, block_x)
    group = jnp.where(centre, jnp.where(off_y == 1, 0, 1), 2)
    alive = lax.broadcasted_iota(jnp.int32, index.shape, 0) < live_ref[...]
    group = jnp.where(alive, group, 3)
    target = lax.broadcasted_iota(jnp.int32, index.shape, 1)
    sum_at, points_at = block * caps + cap, block * nrows * caps + cap
    code_v[0:slots, 0:caps] = (group << 26) + (target << 20) + (sum_at << 10) + points_at
    copy = pltpu.make_async_copy(code_v, code_s, sem)
    copy.start()

    basis_ref[...] = jnp.zeros_like(basis_ref)
    basis_ref[:, 0:npoints] = synth_ref[...]
    points[...] = jnp.zeros_like(points)
    upsampled = jnp.dot(coef_ref[...], basis_ref[...], precision=HIGHEST, preferred_element_type=F32)
    put(points, upsampled)
    reach_ref[0] = farthest(upsampled, caps, 1)
    cots[...] = jnp.zeros_like(cots)
    put(cots, jnp.concatenate([cot_ref[...], jnp.zeros((3 * caps, npts - npoints), F32)], axis=1))
    for t in range(caps):
        p = take(points, t, caps)
        c = take(cots, t, caps)
        target_ref[t] = p
        cotan_ref[t] = c
        w1, w2, w3 = [w.astype(F32) for w in split3(target_factor(p))]
        pad = jnp.zeros((LANES - 6 * ROWS, npts), F32)
        factor_ref[t] = cat(w1, w1, w2, w2, w1, w3, pad).T.astype(BF16)
        c3 = c[0:3]
        a = cat(c3 * p[0:1], c3 * p[1:2], c3 * p[2:3], c3, jnp.zeros((4, npts), F32))
        rows_ref[t] = cat(*split3(a))
    copy.wait()

    def each_slot(k, counts):
        counts = list(counts)
        for t in range(caps):
            code = code_s[k, t]
            which = code >> 26
            n = jnp.where(which == 0, counts[0], jnp.where(which == 1, counts[1], counts[2]))
            list_ref[which, jnp.where(which == 3, 0, n)] = code
            for c in range(3):
                counts[c] += (which == c).astype(jnp.int32)
        return tuple(counts)

    counts = lax.fori_loop(0, slots, each_slot, (jnp.int32(0),) * 3)
    for c in range(3):
        count_ref[c] = counts[c]
    count_ref[3] = 0


def prepare(where, near, live, coef, cot, synth_t, npts):
    slots, caps = near.shape
    nsh = synth_t.shape[0]
    return pl.pallas_call(
        functools.partial(
            prepare_kernel, width_x=lax.axis_size("gx"), width_y=lax.axis_size("gy")
        ),
        out_shape=(
            jax.ShapeDtypeStruct((4, up(slots * caps + LANES, LANES)), jnp.int32),
            jax.ShapeDtypeStruct((4,), jnp.int32),
            jax.ShapeDtypeStruct((1,), F32),
            jax.ShapeDtypeStruct((caps, ROWS, npts), F32),
            jax.ShapeDtypeStruct((caps, npts, LANES), BF16),
            jax.ShapeDtypeStruct((caps, 6 * ROWS, npts), BF16),
            jax.ShapeDtypeStruct((caps, ROWS, npts), F32),
            jax.ShapeDtypeStruct((nsh, npts), F32),
        ),
        in_specs=[SMEM] + [VMEM] * 5,
        out_specs=(SMEM,) * 3 + (VMEM,) * 5,
        scratch_shapes=[
            pltpu.VMEM((up(slots, ROWS), LANES), jnp.int32),
            pltpu.SMEM((up(slots, ROWS), LANES), jnp.int32),
            pltpu.VMEM((npts // LANES, ROWS * caps, LANES), F32),
            pltpu.VMEM((npts // LANES, ROWS * caps, LANES), F32),
            pltpu.SemaphoreType.DMA(()),
        ],
        compiler_params=pltpu.CompilerParams(vmem_limit_bytes=VMEM_LIMIT),
        name="prepare",
    )(where, near, live, coef, cot, synth_t)


def pairs_kernel(which, nsrc, nblocks, list_ref, count_ref, reach_ref, basis_ref, weight_ref, target_hbm, cotan_hbm, factor_hbm, rows_hbm, *rest):
    coef_refs, count_out, out_refs = rest[:nsrc], rest[nsrc], rest[nsrc + 1 : nsrc + 1 + nblocks]
    points, total, base_sc, factor, rows, exact_t, exact_c, column, sems = rest[nsrc + 1 + nblocks :]
    caps, npts, _ = factor.shape
    nsh = basis_ref.shape[0]
    copies = [
        pltpu.make_async_copy(factor_hbm, factor, sems.at[0]),
        pltpu.make_async_copy(rows_hbm, rows, sems.at[1]),
    ]
    for copy in copies:
        copy.start()
    for c in range(4):
        count_out[c] = count_ref[c]
    tiles = [(j, min(TILE, npts - j)) for j in range(0, npts, TILE)]
    total[...] = jnp.zeros_like(total)
    flat = cat(*[ref[...].reshape(-1, nsh) for ref in coef_refs])
    nflat = flat.shape[0]
    block_rows = nflat // nblocks
    upsampled = jnp.dot(flat, basis_ref[...], precision=HIGHEST, preferred_element_type=F32)
    put(points, upsampled)
    points[:, nflat:] = jnp.zeros((points.shape[0], points.shape[1] - nflat, LANES), F32)
    dummy = (nblocks * caps << 10) + nflat
    count = count_ref[which]

    def entry(k):
        code = jnp.where(k < count, list_ref[which, k], dummy)
        return (code >> 20) & 63, (code >> 10) & 1023, code & 1023

    def source_of(at):
        return take(points, at, caps)

    def squares(k):
        t, _, at = entry(k)
        u1, u2, u3 = [u.astype(F32) for u in split3(source_factor(source_of(at)))]
        pad = jnp.zeros((LANES - 6 * ROWS, npts), F32)
        source = cat(u1, u2, u1, u2, u3, u1, pad).astype(BF16)
        for j, jc in tiles:
            base_sc[:, j : j + jc] = jnp.dot(factor[t], source[:, j : j + jc], preferred_element_type=F32)
            yield

    def contract(k):
        t, s, at = entry(k)
        p = source_of(at)
        for j, jc in tiles:
            r = lax.rsqrt(base_sc[:, j : j + jc])
            r3 = r * r * r
            high = r3.astype(BF16)
            low = (r3 - high.astype(F32)).astype(BF16)
            d1 = jnp.dot(rows[t], high, preferred_element_type=F32)
            d2 = jnp.dot(rows[t, 0:32], low, preferred_element_type=F32)
            sums = d1[0:16] + d1[16:32] + d1[32:48] + d2[0:16] + d2[16:32]
            y = p[:, j : j + jc]
            plain = sums[9:12]
            term = y[3:4] * (sums[0:3] - y[0:1] * plain)
            term += y[4:5] * (sums[3:6] - y[1:2] * plain)
            term += y[5:6] * (sums[6:9] - y[2:3] * plain)
            total[s, 0:3, j : j + jc] += term
            yield

    def fast_steps(q, _):
        for z in range(UNROLL):
            now, ahead = contract(q * UNROLL + z), squares(q * UNROLL + z + 1)
            for _ in tiles:
                next(now)
                next(ahead)
        return 0

    def exact_step(k, _):
        t, s, at = entry(k)
        pltpu.sync_copy(target_hbm.at[t], exact_t)
        pltpu.sync_copy(cotan_hbm.at[t], exact_c)
        pad = jnp.zeros((LANES - ROWS, npts), F32)
        column[...] = cat(exact_t[...], pad).T
        y = source_of(at)

        def each_chunk(i, acc):
            start = pl.multiple_of(i * LANES, LANES)
            x = column[pl.ds(start, LANES), :]
            numer, base = 0.0, DELTA_SQ
            for d in range(3):
                differ = x[:, d : d + 1] - y[d : d + 1]
                base = base + differ * differ
                numer = numer + differ * y[3 + d : 4 + d]
            kernel = numer / (base * jnp.sqrt(base))
            cot = exact_c[:, pl.ds(start, LANES)]
            return acc + jnp.dot(cot, kernel, precision=HIGHEST, preferred_element_type=F32)

        term = lax.fori_loop(0, npts // LANES, each_chunk, jnp.zeros((ROWS, npts), F32))
        total[s] += term
        return 0

    for copy in copies:
        copy.wait()
    reach = jnp.maximum(reach_ref[0], farthest(upsampled, caps, nblocks))
    expands = reach <= RADIUS_SQ_MAX

    @pl.when(jnp.logical_and(expands, count > 0))
    def _():
        for _ in squares(0):
            pass
        lax.fori_loop(0, (count + UNROLL - 1) // UNROLL, fast_steps, 0)

    @pl.when(jnp.logical_not(expands))
    def _():
        lax.fori_loop(0, count, exact_step, 0)

    nsum = nblocks * caps
    scaled = (total[0:nsum] * weight_ref[...][None]).reshape(nsum * ROWS, npts)
    contract_last = (((1,), (1,)), ((), ()))
    th, bh = scaled.astype(BF16), basis_ref[...].astype(BF16)
    tl = (scaled - th.astype(F32)).astype(BF16)
    bl = (basis_ref[...] - bh.astype(F32)).astype(BF16)
    grad = lax.dot_general(th, bh, contract_last, preferred_element_type=F32)
    grad += lax.dot_general(tl, bh, contract_last, preferred_element_type=F32)
    grad += lax.dot_general(th, bl, contract_last, preferred_element_type=F32)
    grad = grad.reshape(nblocks, caps, ROWS, nsh)
    for b in range(nblocks):
        for d in range(3):
            out_refs[b][d] = grad[b, :, d]


def pairs(which, name, shared, counts, coefs, nblocks):
    lists, reach, target, factor, rows, cotan, basis, weights = shared
    caps, npts, _ = factor.shape
    nsh = basis.shape[0]
    nflat = sum(c.size for c in coefs) // nsh
    flops = 2 * caps * nblocks * npts * npts * 64
    out = pl.pallas_call(
        functools.partial(pairs_kernel, which, len(coefs), nblocks),
        out_shape=(jax.ShapeDtypeStruct((4,), jnp.int32),)
        + (jax.ShapeDtypeStruct((3, caps, nsh), F32),) * nblocks,
        in_specs=[SMEM] * 3 + [VMEM] * 2 + [ANY] * 4 + [VMEM] * len(coefs),
        out_specs=(SMEM,) + (VMEM,) * nblocks,
        scratch_shapes=[
            pltpu.VMEM((npts // LANES, nflat + ROWS * caps, LANES), F32),
            pltpu.VMEM((nblocks * caps + 1, ROWS, npts), F32),
            pltpu.VMEM((npts, npts), F32),
            pltpu.VMEM(factor.shape, BF16),
            pltpu.VMEM(rows.shape, BF16),
            pltpu.VMEM((ROWS, npts), F32),
            pltpu.VMEM((ROWS, npts), F32),
            pltpu.VMEM((npts, LANES), F32),
            pltpu.SemaphoreType.DMA((2,)),
        ],
        cost_estimate=pl.CostEstimate(flops=flops, bytes_accessed=1 << 22, transcendentals=0),
        compiler_params=pltpu.CompilerParams(vmem_limit_bytes=VMEM_LIMIT),
        name=name,
    )(lists, counts, reach, basis, weights, target, cotan, factor, rows, *coefs)
    return out[0], out[1:]


def shards(shape_coef, cotangent, neighbours, counts, synth, weights, stiffness):
    caps, nrows, nsh = shape_coef.shape[2:]
    npoints = synth.shape[0]
    npts = up(npoints, LANES)
    where = jnp.stack([lax.axis_index("gx"), lax.axis_index("gy")]).astype(jnp.int32)

    coef = shape_coef[0, 0].transpose(1, 0, 2).reshape(nrows * caps, nsh)
    from_below = shifted(coef, "gy", 1)
    from_above = shifted(coef, "gy", -1)
    column = jnp.stack([from_below, coef, from_above])
    from_left = shifted(column, "gx", 1)
    from_right = shifted(column, "gx", -1)

    cot = cotangent[0, 0].transpose(1, 0, 2).reshape(3 * caps, npoints)
    weight_pad = jnp.pad(weights, (0, npts - npoints)).reshape(1, npts)
    near = neighbours[0, 0].T
    lists, live, *arrays = prepare(where, near, counts[0], coef, cot, synth.T, npts)
    shared = (lists, *arrays, weight_pad)

    live, (below, above) = pairs(1, "pairs_gy", shared, live, [from_below, from_above], 2)
    grad = moved(below, 0, -1) + moved(above, 0, 1)
    live, sides = pairs(2, "pairs_gx", shared, live, [from_left, from_right], 6)
    places = [(dx, dy) for dx in (-1, 1) for dy in (-1, 0, 1)]
    arrived = [moved(part, dx, dy) for part, (dx, dy) in zip(sides, places)]
    live, (mine,) = pairs(0, "pairs_local", shared, live, [coef], 1)
    grad = functools.reduce(jnp.add, arrived, grad + mine) * stiffness
    return grad.transpose(1, 0, 2)[None, None]


def solution(mesh):
    placed = (
        P("gx", "gy", None, None, None),
        P("gx", "gy", None, None, None),
        P("gx", "gy", None, None),
        P("gx", "gy", None),
        P(),
        P(),
        P(),
    )
    return jax.shard_map(
        shards,
        mesh=mesh,
        in_specs=placed,
        out_specs=P("gx", "gy", None, None, None),
        check_vma=False,
    )
```

```python
import functools

import jax
import jax.numpy as jnp
from jax import lax
from jax.experimental import pallas as pl
from jax.experimental.pallas import tpu as pltpu
from jax.sharding import PartitionSpec as P


F32, BF16 = jnp.float32, jnp.bfloat16
DELTA_SQ = 0.0625
RADIUS_SQ_MAX = 64.0
HIGHEST = lax.Precision.HIGHEST
LANES = 128
ROWS = 8
VMEM_LIMIT = 28 << 20
TILE = 256
UNROLL = 2
VMEM = pl.BlockSpec(memory_space=pltpu.VMEM)
SMEM = pl.BlockSpec(memory_space=pltpu.SMEM)


def up(n, m):
    return -(-n // m) * m


def shifted(block, axis, distance):
    devices = range(lax.axis_size(axis))
    route = [((i - distance) % len(devices), i) for i in devices]
    return lax.ppermute(block, axis, route)


def moved(block, dx, dy):
    wx, wy = lax.axis_size("gx"), lax.axis_size("gy")
    grid = [(x, y) for x in range(wx) for y in range(wy)]
    route = [(x * wy + y, (x + dx) % wx * wy + (y + dy) % wy) for x, y in grid]
    return lax.ppermute(block, ("gx", "gy"), route)


def put(ref, value):
    for lane in range(ref.shape[0]):
        ref[lane, 0 : value.shape[0]] = value[:, lane * LANES : (lane + 1) * LANES]


def take(ref, at, stride):
    parts = [ref[lane, pl.ds(at, ROWS, stride=stride), :] for lane in range(ref.shape[0])]
    return jnp.concatenate(parts, axis=1)


def farthest(rows, caps, nblocks):
    sizes = []
    for start in range(0, rows.shape[0], rows.shape[0] // nblocks):
        x, y, z = [rows[at : at + caps] for at in range(start, start + 3 * caps, caps)]
        sizes.append(x * x + y * y + z * z)
    return jnp.max(functools.reduce(jnp.maximum, sizes))


def quotient(v, n):
    return v >> (n.bit_length() - 1) if n & (n - 1) == 0 else lax.div(v, jnp.int32(n))


def offset(block, here, width):
    step = block - here + 1
    return jnp.where(step < 0, step + width, jnp.where(step >= width, step - width, step))


def list_length(entries):
    return up(entries + ROWS, LANES)


def split3(v):
    high = v.astype(BF16)
    rest = v - high.astype(F32)
    mid = rest.astype(BF16)
    return high, mid, (rest - mid.astype(F32)).astype(BF16)


def cat(*xs):
    return jnp.concatenate(xs, axis=0)


def square(p):
    return p[0:1] * p[0:1] + p[1:2] * p[1:2] + p[2:3] * p[2:3]


def target_factor(p):
    row = lax.broadcasted_iota(jnp.int32, p.shape, 0)
    tail = jnp.where(row == 4, square(p) + DELTA_SQ, 0.0)
    return jnp.where(row < 3, p, jnp.where(row == 3, 1.0, tail))


def source_factor(p):
    row = lax.broadcasted_iota(jnp.int32, p.shape, 0)
    tail = jnp.where(row == 4, 1.0, 0.0)
    return jnp.where(row < 3, -2.0 * p, jnp.where(row == 3, square(p), tail))


def prepare_kernel(
    where_ref, near_ref, live_ref, coef_ref, cot_ref, synth_ref,
    list_ref, count_ref, reach_ref, target_ref, factor_ref, rows_ref, cotan_ref, basis_ref, mine_ref,
    near_v, plan_v, plan_s, points, cots, sem, *, width_x, width_y,
):
    slots, caps = near_ref.shape
    nsh, npoints = synth_ref.shape
    npts = basis_ref.shape[1]
    nrows = coef_ref.shape[0] // caps

    held = near_v.shape[0]
    length = list_length(slots * caps)
    near_v[...] = jnp.zeros_like(near_v)
    near_v[0:slots, 0:caps] = near_ref[...]
    near_v[held - 1 :, 0:caps] = live_ref[...]
    index = near_v[...]
    row = lax.broadcasted_iota(jnp.int32, index.shape, 0)
    target = lax.broadcasted_iota(jnp.int32, index.shape, 1)
    column = quotient(index, caps)
    line = quotient(column, width_y)
    cap = index - column * caps
    off_x = offset(line, where_ref[0], width_x)
    off_y = offset(column - line * width_y, where_ref[1], width_y)
    block_x = jnp.where(off_x == 2, 3, 0) + off_y
    block_y = jnp.where(off_y == 2, 1, 0)
    centre = off_x == 1
    block = jnp.where(centre, jnp.where(off_y == 1, 0, block_y), block_x)
    group = jnp.where(centre, jnp.where(off_y == 1, 0, 1), 2)
    alive = jnp.logical_and(row < index[held - 1 :], jnp.logical_and(row < slots, target < caps))
    group = jnp.where(alive, group, 3)
    sum_at, points_at = block * caps + cap, block * nrows * caps + cap
    marks = cat(*[jnp.where(group == g, 1.0, 0.0) for g in range(3)]).astype(BF16)
    before = lax.broadcasted_iota(jnp.int32, (LANES, LANES), 0) < lax.broadcasted_iota(jnp.int32, (LANES, LANES), 1)
    ranks = jnp.dot(marks, before.astype(F32).astype(BF16), preferred_element_type=F32)
    sums = jnp.dot(marks, jnp.ones((LANES, LANES), BF16), preferred_element_type=F32)
    i = lax.broadcasted_iota(jnp.int32, (3 * held, 3 * held), 0)
    j = lax.broadcasted_iota(jnp.int32, (3 * held, 3 * held), 1)
    above = jnp.logical_and(j < i, quotient(i, held) == quotient(j, held))
    starts = jnp.dot(above.astype(F32).astype(BF16), sums.astype(BF16), preferred_element_type=F32)
    ranks = (ranks + starts).astype(jnp.int32)
    place = 3 * length
    for g in range(3):
        place = jnp.where(group == g, g * length + ranks[g * held : (g + 1) * held], place)
    plan_v[0:held] = (target << 20) + (sum_at << 10) + points_at
    plan_v[held : 2 * held] = place
    plan_v[2 * held :] = starts.astype(jnp.int32)
    copy = pltpu.make_async_copy(plan_v, plan_s, sem)
    copy.start()

    mine_ref[...] = coef_ref[...]
    basis_ref[...] = jnp.zeros_like(basis_ref)
    basis_ref[:, 0:npoints] = synth_ref[...]
    points[...] = jnp.zeros_like(points)
    upsampled = jnp.dot(coef_ref[...], basis_ref[...], precision=HIGHEST, preferred_element_type=F32)
    put(points, upsampled)
    reach_ref[0] = farthest(upsampled, caps, 1)
    cots[...] = jnp.zeros_like(cots)
    put(cots, jnp.concatenate([cot_ref[...], jnp.zeros((3 * caps, npts - npoints), F32)], axis=1))
    for t in range(caps):
        p = take(points, t, caps)
        c = take(cots, t, caps)
        target_ref[t] = p
        cotan_ref[t] = c
        w1, w2, w3 = [w.astype(F32) for w in split3(target_factor(p))]
        pad = jnp.zeros((LANES - 6 * ROWS, npts), F32)
        factor_ref[t] = cat(w1, w1, w2, w2, w1, w3, pad).T.astype(BF16)
        c3 = c[0:3]
        a = cat(c3 * p[0:1], c3 * p[1:2], c3 * p[2:3], c3, jnp.zeros((4, npts), F32))
        rows_ref[t] = cat(*split3(a))
    copy.wait()

    def each_slot(k, _):
        for t in range(caps):
            list_ref[plan_s[held + k, t]] = plan_s[k, t]
        return 0

    lax.fori_loop(0, slots, each_slot, 0)
    for g in range(3):
        count_ref[g] = plan_s[(g + 3) * held - 1, 0]
    count_ref[3] = 0


def prepare(where, near, live, coef, cot, synth_t, npts):
    slots, caps = near.shape
    nsh = synth_t.shape[0]
    held = up(slots + 1, ROWS)
    return pl.pallas_call(
        functools.partial(
            prepare_kernel, width_x=lax.axis_size("gx"), width_y=lax.axis_size("gy")
        ),
        out_shape=(
            jax.ShapeDtypeStruct((3 * list_length(slots * caps) + LANES,), jnp.int32),
            jax.ShapeDtypeStruct((4,), jnp.int32),
            jax.ShapeDtypeStruct((1,), F32),
            jax.ShapeDtypeStruct((caps, ROWS, npts), F32),
            jax.ShapeDtypeStruct((caps, npts, LANES), BF16),
            jax.ShapeDtypeStruct((caps, 6 * ROWS, npts), BF16),
            jax.ShapeDtypeStruct((caps, ROWS, npts), F32),
            jax.ShapeDtypeStruct((nsh, npts), F32),
            jax.ShapeDtypeStruct(coef.shape, F32),
        ),
        in_specs=[SMEM] + [VMEM] * 5,
        out_specs=(SMEM,) * 3 + (VMEM,) * 6,
        scratch_shapes=[
            pltpu.VMEM((held, LANES), jnp.int32),
            pltpu.VMEM((5 * held, LANES), jnp.int32),
            pltpu.SMEM((5 * held, LANES), jnp.int32),
            pltpu.VMEM((npts // LANES, ROWS * caps, LANES), F32),
            pltpu.VMEM((npts // LANES, ROWS * caps, LANES), F32),
            pltpu.SemaphoreType.DMA(()),
        ],
        compiler_params=pltpu.CompilerParams(vmem_limit_bytes=VMEM_LIMIT),
        name="prepare",
    )(where, near, live, coef, cot, synth_t)


def pairs_kernel(which, nsrc, nblocks, list_ref, count_ref, reach_ref, basis_ref, weight_ref, target_ref, cotan_ref, factor, rows, *rest):
    coef_refs, count_out, out_refs = rest[:nsrc], rest[nsrc], rest[nsrc + 1 : nsrc + 1 + nblocks]
    points, total, base_sc, column = rest[nsrc + 1 + nblocks :]
    caps, npts, _ = factor.shape
    nsh = basis_ref.shape[0]
    for c in range(4):
        count_out[c] = count_ref[c]
    tiles = [(j, min(TILE, npts - j)) for j in range(0, npts, TILE)]
    total[...] = jnp.zeros_like(total)
    flat = cat(*[ref[...].reshape(-1, nsh) for ref in coef_refs])
    nflat = flat.shape[0]
    block_rows = nflat // nblocks
    upsampled = jnp.dot(flat, basis_ref[...], precision=HIGHEST, preferred_element_type=F32)
    put(points, upsampled)
    points[:, nflat:] = jnp.zeros((points.shape[0], points.shape[1] - nflat, LANES), F32)
    dummy = (nblocks * caps << 10) + nflat
    count = count_ref[which]
    start = which * (list_ref.shape[0] // 3 // LANES * LANES)

    def entry(k):
        code = jnp.where(k < count, list_ref[start + k], dummy)
        return (code >> 20) & 63, (code >> 10) & 1023, code & 1023

    def source_of(at):
        return take(points, at, caps)

    def squares(k):
        t, _, at = entry(k)
        u1, u2, u3 = [u.astype(F32) for u in split3(source_factor(source_of(at)))]
        pad = jnp.zeros((LANES - 6 * ROWS, npts), F32)
        source = cat(u1, u2, u1, u2, u3, u1, pad).astype(BF16)
        for j, jc in tiles:
            base_sc[:, j : j + jc] = jnp.dot(factor[t], source[:, j : j + jc], preferred_element_type=F32)
            yield

    def contract(k):
        t, s, at = entry(k)
        p = source_of(at)
        for j, jc in tiles:
            r = lax.rsqrt(base_sc[:, j : j + jc])
            r3 = r * r * r
            high = r3.astype(BF16)
            low = (r3 - high.astype(F32)).astype(BF16)
            d1 = jnp.dot(rows[t], high, preferred_element_type=F32)
            d2 = jnp.dot(rows[t, 0:32], low, preferred_element_type=F32)
            sums = d1[0:16] + d1[16:32] + d1[32:48] + d2[0:16] + d2[16:32]
            y = p[:, j : j + jc]
            plain = sums[9:12]
            term = y[3:4] * (sums[0:3] - y[0:1] * plain)
            term += y[4:5] * (sums[3:6] - y[1:2] * plain)
            term += y[5:6] * (sums[6:9] - y[2:3] * plain)
            for lane in range(j // LANES, (j + jc) // LANES):
                part = term[:, lane * LANES - j : (lane + 1) * LANES - j]
                total[lane, pl.ds(pl.multiple_of(s * ROWS, ROWS), 3), :] += part
            yield

    def fast_steps(q, _):
        for z in range(UNROLL):
            now, ahead = contract(q * UNROLL + z), squares(q * UNROLL + z + 1)
            for _ in tiles:
                next(now)
                next(ahead)
        return 0

    def exact_step(k, _):
        t, s, at = entry(k)
        pad = jnp.zeros((LANES - ROWS, npts), F32)
        column[...] = cat(target_ref[t], pad).T
        y = source_of(at)

        def each_chunk(i, acc):
            start = pl.multiple_of(i * LANES, LANES)
            x = column[pl.ds(start, LANES), :]
            numer, base = 0.0, DELTA_SQ
            for d in range(3):
                differ = x[:, d : d + 1] - y[d : d + 1]
                base = base + differ * differ
                numer = numer + differ * y[3 + d : 4 + d]
            kernel = numer / (base * jnp.sqrt(base))
            cot = cotan_ref[t, :, pl.ds(start, LANES)]
            return acc + jnp.dot(cot, kernel, precision=HIGHEST, preferred_element_type=F32)

        term = lax.fori_loop(0, npts // LANES, each_chunk, jnp.zeros((ROWS, npts), F32))
        for lane in range(npts // LANES):
            at_sum = pl.ds(pl.multiple_of(s * ROWS, ROWS), ROWS)
            total[lane, at_sum, :] += term[:, lane * LANES : (lane + 1) * LANES]
        return 0

    reach = jnp.maximum(reach_ref[0], farthest(upsampled, caps, nblocks))
    expands = reach <= RADIUS_SQ_MAX

    @pl.when(jnp.logical_and(expands, count > 0))
    def _():
        for _ in squares(0):
            pass
        lax.fori_loop(0, (count + UNROLL - 1) // UNROLL, fast_steps, 0)

    @pl.when(jnp.logical_not(expands))
    def _():
        lax.fori_loop(0, count, exact_step, 0)

    nsum = nblocks * caps
    dense = cat(*[
        jnp.concatenate([total[lane, pl.ds(d, nsum, stride=ROWS), :] for lane in range(npts // LANES)], axis=1)
        for d in range(3)
    ])
    scaled = dense * weight_ref[...]
    contract_last = (((1,), (1,)), ((), ()))
    th, bh = scaled.astype(BF16), basis_ref[...].astype(BF16)
    tl = (scaled - th.astype(F32)).astype(BF16)
    bl = (basis_ref[...] - bh.astype(F32)).astype(BF16)
    grad = lax.dot_general(th, bh, contract_last, preferred_element_type=F32)
    grad += lax.dot_general(tl, bh, contract_last, preferred_element_type=F32)
    grad += lax.dot_general(th, bl, contract_last, preferred_element_type=F32)
    for b in range(nblocks):
        for d in range(3):
            at = d * nsum + b * caps
            out_refs[b][d] = grad[at : at + caps]


def pairs(which, name, shared, counts, coefs, nblocks):
    lists, reach, target, factor, rows, cotan, basis, weights = shared
    caps, npts, _ = factor.shape
    nsh = basis.shape[0]
    nflat = sum(c.size for c in coefs) // nsh
    flops = 2 * caps * nblocks * npts * npts * 64
    out = pl.pallas_call(
        functools.partial(pairs_kernel, which, len(coefs), nblocks),
        out_shape=(jax.ShapeDtypeStruct((4,), jnp.int32),)
        + (jax.ShapeDtypeStruct((3, caps, nsh), F32),) * nblocks,
        in_specs=[SMEM] * 3 + [VMEM] * (6 + len(coefs)),
        out_specs=(SMEM,) + (VMEM,) * nblocks,
        scratch_shapes=[
            pltpu.VMEM((npts // LANES, nflat + ROWS * caps, LANES), F32),
            pltpu.VMEM((npts // LANES, (nblocks * caps + 1) * ROWS, LANES), F32),
            pltpu.VMEM((npts, npts), F32),
            pltpu.VMEM((npts, LANES), F32),
        ],
        cost_estimate=pl.CostEstimate(flops=flops, bytes_accessed=1 << 22, transcendentals=0),
        compiler_params=pltpu.CompilerParams(vmem_limit_bytes=VMEM_LIMIT),
        name=name,
    )(lists, counts, reach, basis, weights, target, cotan, factor, rows, *coefs)
    return out[0], out[1:]


def shards(shape_coef, cotangent, neighbours, counts, synth, weights, stiffness):
    caps, nrows, nsh = shape_coef.shape[2:]
    npoints = synth.shape[0]
    npts = up(npoints, LANES)
    where = jnp.stack([lax.axis_index("gx"), lax.axis_index("gy")]).astype(jnp.int32)

    coef = shape_coef[0, 0].transpose(1, 0, 2).reshape(nrows * caps, nsh)
    from_below = shifted(coef, "gy", 1)
    from_above = shifted(coef, "gy", -1)
    cot = cotangent[0, 0].transpose(1, 0, 2).reshape(3 * caps, npoints)
    weight_pad = jnp.pad(weights, (0, npts - npoints)).reshape(1, npts)
    near = neighbours[0, 0].T
    lists, live, *arrays, mine = prepare(where, near, counts[0], coef, cot, synth.T, npts)
    column = jnp.stack([from_below, mine, from_above])
    from_left = shifted(column, "gx", 1)
    from_right = shifted(column, "gx", -1)
    shared = (lists, *arrays, weight_pad)

    live, inner = pairs(1, "pairs_gy", shared, live, [from_below, from_above], 2)
    live, outer = pairs(2, "pairs_gx", shared, live, [from_left, from_right], 6)
    parts = lax.optimization_barrier((*inner, *outer))
    places = [(0, -1), (0, 1)] + [(dx, dy) for dx in (-1, 1) for dy in (-1, 0, 1)]
    arrived = [moved(part, dx, dy) for part, (dx, dy) in zip(parts, places)]
    live, (grad,) = pairs(0, "pairs_local", shared, live, [mine], 1)
    grad = functools.reduce(jnp.add, arrived, grad) * stiffness
    return grad.transpose(1, 0, 2)[None, None]


def solution(mesh):
    placed = (
        P("gx", "gy", None, None, None),
        P("gx", "gy", None, None, None),
        P("gx", "gy", None, None),
        P("gx", "gy", None),
        P(),
        P(),
        P(),
    )
    return jax.shard_map(
        shards,
        mesh=mesh,
        in_specs=placed,
        out_specs=P("gx", "gy", None, None, None),
        check_vma=False,
    )
```

```python
import functools

import jax
import jax.numpy as jnp
from jax import lax
from jax.experimental import pallas as pl
from jax.experimental.pallas import tpu as pltpu
from jax.sharding import PartitionSpec as P


F32, BF16 = jnp.float32, jnp.bfloat16
DELTA_SQ = 0.0625
RADIUS_SQ_MAX = 64.0
HIGHEST = lax.Precision.HIGHEST
LANES = 128
ROWS = 8
VMEM_LIMIT = 28 << 20
TILE = 256
UNROLL = 2
VMEM = pl.BlockSpec(memory_space=pltpu.VMEM)
SMEM = pl.BlockSpec(memory_space=pltpu.SMEM)


def up(n, m):
    return -(-n // m) * m


def shifted(block, axis, distance):
    devices = range(lax.axis_size(axis))
    route = [((i - distance) % len(devices), i) for i in devices]
    return lax.ppermute(block, axis, route)


def put(ref, value):
    for lane in range(ref.shape[0]):
        ref[lane, 0 : value.shape[0]] = value[:, lane * LANES : (lane + 1) * LANES]


def take(ref, at, stride):
    parts = [ref[lane, pl.ds(at, ROWS, stride=stride), :] for lane in range(ref.shape[0])]
    return jnp.concatenate(parts, axis=1)


def farthest(rows, caps, nblocks):
    sizes = []
    for start in range(0, rows.shape[0], rows.shape[0] // nblocks):
        x, y, z = [rows[at : at + caps] for at in range(start, start + 3 * caps, caps)]
        sizes.append(x * x + y * y + z * z)
    return jnp.max(functools.reduce(jnp.maximum, sizes))


def quotient(v, n):
    return v >> (n.bit_length() - 1) if n & (n - 1) == 0 else lax.div(v, jnp.int32(n))


def offset(block, here, width):
    step = block - here + 1
    return jnp.where(step < 0, step + width, jnp.where(step >= width, step - width, step))


def split3(v):
    high = v.astype(BF16)
    rest = v - high.astype(F32)
    mid = rest.astype(BF16)
    return high, mid, (rest - mid.astype(F32)).astype(BF16)


def cat(*xs):
    return jnp.concatenate(xs, axis=0)


def square(p):
    return p[0:1] * p[0:1] + p[1:2] * p[1:2] + p[2:3] * p[2:3]


def target_factor(p):
    row = lax.broadcasted_iota(jnp.int32, p.shape, 0)
    tail = jnp.where(row == 4, square(p) + DELTA_SQ, 0.0)
    return jnp.where(row < 3, p, jnp.where(row == 3, 1.0, tail))


def source_factor(p):
    row = lax.broadcasted_iota(jnp.int32, p.shape, 0)
    tail = jnp.where(row == 4, 1.0, 0.0)
    return jnp.where(row < 3, -2.0 * p, jnp.where(row == 3, square(p), tail))


def message_kernel(where_ref, near_ref, live_ref, coef_ref, cot_ref, out_ref, near_v, live_v, *, width_x, width_y):
    caps, slots = near_ref.shape
    points, nsh = cot_ref.shape[1], coef_ref.shape[1]
    body = 3 * caps
    near_v[...] = jnp.zeros_like(near_v)
    near_v[:, 0:slots] = near_ref[...]
    live_v[...] = jnp.zeros_like(live_v)
    live_v[0:1, 0:caps] = live_ref[...]
    index = near_v[...]
    target = lax.broadcasted_iota(jnp.int32, index.shape, 0)
    slot = lax.broadcasted_iota(jnp.int32, index.shape, 1)
    counts = jnp.where(target == slot, live_v[0:1], 0).astype(F32)
    counts = jnp.sum(counts, axis=1, keepdims=True)
    column = quotient(index, caps)
    line = quotient(column, width_y)
    cap = index - column * caps
    off_x = offset(line, where_ref[0], width_x)
    off_y = offset(column - line * width_y, where_ref[1], width_y)
    alive = jnp.logical_and(slot.astype(F32) < counts, slot < slots)
    group = jnp.where(alive, off_x * 3 + off_y, 9)
    marks = cat(*[jnp.where(group == g, 1.0, 0.0) for g in range(9)]).astype(BF16)
    row = lax.broadcasted_iota(jnp.int32, (LANES, LANES), 0)
    col = lax.broadcasted_iota(jnp.int32, (LANES, LANES), 1)
    before = jnp.where(row < col, 1.0, 0.0).astype(BF16)
    ranks = jnp.dot(marks, before, preferred_element_type=F32)
    sums = jnp.dot(marks, jnp.ones((LANES, LANES), BF16), preferred_element_type=F32)
    row = lax.broadcasted_iota(jnp.int32, (9 * caps, 9 * caps), 0)
    col = lax.broadcasted_iota(jnp.int32, (9 * caps, 9 * caps), 1)
    above = jnp.where(col < row, 1.0, 0.0).astype(BF16)
    starts = jnp.dot(above, sums.astype(BF16), preferred_element_type=F32)
    ranks += starts
    place = jnp.full(index.shape, -1.0, F32)
    for g in range(9):
        place = jnp.where(group == g, ranks[g * caps : (g + 1) * caps], place)
    code = (target * caps + cap).astype(F32)
    length = up(slots * caps, LANES)
    at = lax.broadcasted_iota(jnp.int32, (caps, length), 1).astype(F32)
    listed = jnp.zeros((caps, length), F32)
    for k in range(slots):
        listed += jnp.where(place[:, k : k + 1] == at, code[:, k : k + 1], 0.0)
    bounds = jnp.zeros((1, LANES), F32)
    for g in range(9):
        bounds = jnp.where(slot[0:1] == g, starts[g * caps : g * caps + 1], bounds)
    last = 9 * caps - 1
    bounds = jnp.where(slot[0:1] == 9, starts[last:] + sums[last:], bounds)

    out_ref[...] = jnp.zeros_like(out_ref)
    out_ref[0:body, 0:points] = cot_ref[...]
    wide = up(points, LANES)
    out_ref[0:body, wide : wide + nsh] = coef_ref[0:body, :]
    out_ref[body : body + 1, 0:length] = jnp.sum(listed, axis=0, keepdims=True)
    out_ref[body + 1 : body + 2, 0:LANES] = bounds


def message(where, near, live, coef, cot, npts):
    caps, slots = near.shape
    width = npts + up(coef.shape[1], LANES)
    return pl.pallas_call(
        functools.partial(message_kernel, width_x=lax.axis_size("gx"), width_y=lax.axis_size("gy")),
        out_shape=jax.ShapeDtypeStruct((3 * caps + ROWS, width), F32),
        in_specs=[SMEM] + [VMEM] * 4,
        out_specs=VMEM,
        scratch_shapes=[pltpu.VMEM((caps, LANES), jnp.int32), pltpu.VMEM((ROWS, LANES), jnp.int32)],
        compiler_params=pltpu.CompilerParams(vmem_limit_bytes=VMEM_LIMIT),
        name="message",
    )(where, near, live, coef, cot)


def sources_kernel(coef_ref, synth_ref, basis_ref, factor_ref, source_ref, reach_ref, points, *, caps):
    npoints, npts = synth_ref.shape[1], basis_ref.shape[1]
    basis_ref[...] = jnp.zeros_like(basis_ref)
    basis_ref[:, 0:npoints] = synth_ref[...]
    upsampled = jnp.dot(coef_ref[...], basis_ref[...], precision=HIGHEST, preferred_element_type=F32)
    points[...] = jnp.zeros_like(points)
    put(points, upsampled)
    reach_ref[0] = farthest(upsampled, caps, 1)
    pad = jnp.zeros((LANES - 6 * ROWS, npts), F32)
    for s in range(caps):
        p = take(points, s, caps)
        source_ref[s] = p
        u1, u2, u3 = [u.astype(F32) for u in split3(source_factor(p))]
        factor_ref[s] = cat(u1, u2, u1, u2, u3, u1, pad).astype(BF16)


def sources(coef, synth_t, npts, caps):
    return pl.pallas_call(
        functools.partial(sources_kernel, caps=caps),
        out_shape=(
            jax.ShapeDtypeStruct((synth_t.shape[0], npts), F32),
            jax.ShapeDtypeStruct((caps, LANES, npts), BF16),
            jax.ShapeDtypeStruct((caps, ROWS, npts), F32),
            jax.ShapeDtypeStruct((1,), F32),
        ),
        in_specs=[VMEM] * 2,
        out_specs=(VMEM, VMEM, VMEM, SMEM),
        scratch_shapes=[pltpu.VMEM((npts // LANES, ROWS * caps, LANES), F32)],
        compiler_params=pltpu.CompilerParams(vmem_limit_bytes=VMEM_LIMIT),
        name="sources",
    )(coef, synth_t)


def pairs_kernel(groups, nmsg, final, reach_ref, basis_ref, factor_ref, source_ref, *rest):
    msg_refs, rest = rest[:nmsg], rest[nmsg:]
    if final:
        begun_ref, weight_ref, stiff_ref, out_ref, *scratch = rest
    else:
        out_ref, *scratch = rest
    points, cots, base_sc, target_f, total, plan_v, plan_s, entries, column, sem = scratch
    caps, _, npts = source_ref.shape
    nsh = basis_ref.shape[0]
    nblocks, body = len(groups), 3 * caps
    tiles = [(j, min(TILE, npts - j)) for j in range(0, npts, TILE)]
    messages = [ref.at[i] for ref in msg_refs for i in range(ref.shape[0])]

    length = plan_v.shape[1]
    for b, msg in enumerate(messages):
        plan_v[b * ROWS : (b + 1) * ROWS] = msg[body : body + ROWS, 0:length].astype(jnp.int32)
    copy = pltpu.make_async_copy(plan_v, plan_s, sem)
    copy.start()
    total[...] = begun_ref[...] if final else jnp.zeros_like(total)
    flat = cat(*[msg[0:body, npts : npts + nsh] for msg in messages])
    upsampled = jnp.dot(flat, basis_ref[...], precision=HIGHEST, preferred_element_type=F32)
    put(points, upsampled)
    put(cots, cat(*[msg[0:body, 0:npts] for msg in messages]))
    for ref in (points, cots):
        ref[:, nblocks * body :] = jnp.zeros((ref.shape[0], ref.shape[1] - nblocks * body, LANES), F32)
    copy.wait()

    count = jnp.int32(0)
    for b, g in enumerate(groups):
        first, end = plan_s[b * ROWS + 1, g], plan_s[b * ROWS + 1, g + 1]

        def copy_entry(k, _):
            code = plan_s[b * ROWS, k]
            t = quotient(code, caps)
            entries[count + k - first] = ((b * body + t) << 8) + code - t * caps
            return 0

        lax.fori_loop(first, end, copy_entry, 0)
        count += end - first

    def entry(k):
        inside = k < count
        code = jnp.where(inside, entries[k], 0)
        s = code & 255
        return code >> 8, s, jnp.where(inside, s, caps)

    def squares(k, held):
        at, s, _ = entry(k)
        w1, w2, w3 = [w.astype(F32) for w in split3(target_factor(take(points, at, caps)))]
        pad = jnp.zeros((LANES - 6 * ROWS, npts), F32)
        target_f[held] = cat(w1, w1, w2, w2, w1, w3, pad).T.astype(BF16)
        for j, jc in tiles:
            base_sc[:, j : j + jc] = jnp.dot(
                target_f[held], factor_ref[s, :, j : j + jc], preferred_element_type=F32
            )
            yield

    def contract(k):
        at, s, sum_at = entry(k)
        p, c3 = take(points, at, caps), take(cots, at, caps)[0:3]
        a = cat(c3 * p[0:1], c3 * p[1:2], c3 * p[2:3], c3, jnp.zeros((4, npts), F32))
        rows = cat(*split3(a))
        for j, jc in tiles:
            r = lax.rsqrt(base_sc[:, j : j + jc])
            r3 = r * r * r
            high = r3.astype(BF16)
            low = (r3 - high.astype(F32)).astype(BF16)
            d1 = jnp.dot(rows, high, preferred_element_type=F32)
            d2 = jnp.dot(rows[0:32], low, preferred_element_type=F32)
            sums = d1[0:16] + d1[16:32] + d1[32:48] + d2[0:16] + d2[16:32]
            y = source_ref[s, :, j : j + jc]
            plain = sums[9:12]
            term = y[3:4] * (sums[0:3] - y[0:1] * plain)
            term += y[4:5] * (sums[3:6] - y[1:2] * plain)
            term += y[5:6] * (sums[6:9] - y[2:3] * plain)
            for lane in range(j // LANES, (j + jc) // LANES):
                part = term[:, lane * LANES - j : (lane + 1) * LANES - j]
                total[lane, pl.ds(pl.multiple_of(sum_at * ROWS, ROWS), 3), :] += part
            yield

    def fast_steps(q, _):
        for z in range(UNROLL):
            k = q * UNROLL + z
            now, ahead = contract(k), squares(k + 1, z % 2)
            for _ in tiles:
                next(now)
                next(ahead)
        return 0

    def exact_step(k, _):
        at, s, sum_at = entry(k)
        pad = jnp.zeros((LANES - ROWS, npts), F32)
        column[0] = cat(take(points, at, caps), pad).T
        column[1] = cat(take(cots, at, caps), pad).T
        y = source_ref[s]

        def each_chunk(i, acc):
            start = pl.multiple_of(i * LANES, LANES)
            x = column[0, pl.ds(start, LANES), :]
            numer, base = 0.0, DELTA_SQ
            for d in range(3):
                differ = x[:, d : d + 1] - y[d : d + 1]
                base = base + differ * differ
                numer = numer + differ * y[3 + d : 4 + d]
            kernel = numer / (base * jnp.sqrt(base))
            cot = column[1, pl.ds(start, LANES), :].T[0:ROWS]
            return acc + jnp.dot(cot, kernel, precision=HIGHEST, preferred_element_type=F32)

        term = lax.fori_loop(0, npts // LANES, each_chunk, jnp.zeros((ROWS, npts), F32))
        for lane in range(npts // LANES):
            part = term[0:3, lane * LANES : (lane + 1) * LANES]
            total[lane, pl.ds(pl.multiple_of(sum_at * ROWS, ROWS), 3), :] += part
        return 0

    reach = jnp.maximum(reach_ref[0], farthest(upsampled, caps, nblocks))
    expands = reach <= RADIUS_SQ_MAX

    @pl.when(jnp.logical_and(expands, count > 0))
    def _():
        for _ in squares(0, 1):
            pass
        lax.fori_loop(0, (count + UNROLL - 1) // UNROLL, fast_steps, 0)

    @pl.when(jnp.logical_not(expands))
    def _():
        lax.fori_loop(0, count, exact_step, 0)

    if not final:
        out_ref[...] = total[...]
        return
    dense = cat(*[
        jnp.concatenate([total[lane, pl.ds(d, caps, stride=ROWS), :] for lane in range(npts // LANES)], axis=1)
        for d in range(3)
    ])
    scaled = dense * weight_ref[...]
    grad = lax.dot_general(
        scaled, basis_ref[...], (((1,), (1,)), ((), ())), precision=HIGHEST, preferred_element_type=F32
    )
    out_ref[...] = (grad * stiff_ref[...]).reshape(3, caps, nsh)


def pairs(name, groups, prepared, slots, messages, begun=None):
    basis, factor, source, reach = prepared
    caps, _, npts = source.shape
    nsh = basis.shape[0]
    nblocks, lanes = len(groups), npts // LANES
    final = begun is not None
    total = jax.ShapeDtypeStruct((lanes, (caps + 1) * ROWS, LANES), F32)
    out = jax.ShapeDtypeStruct((3, caps, nsh), F32) if final else total
    held = nblocks * 3 * caps + ROWS * caps
    flops = 2 * caps * nblocks * npts * npts * 64
    extra = tuple(begun) if final else ()
    return pl.pallas_call(
        functools.partial(pairs_kernel, groups, len(messages), final),
        out_shape=out,
        in_specs=[SMEM] + [VMEM] * (3 + len(messages) + len(extra)),
        out_specs=VMEM,
        scratch_shapes=[
            pltpu.VMEM((lanes, held, LANES), F32),
            pltpu.VMEM((lanes, held, LANES), F32),
            pltpu.VMEM((npts, npts), F32),
            pltpu.VMEM((2, npts, LANES), BF16),
            pltpu.VMEM(total.shape, F32),
            pltpu.VMEM((nblocks * ROWS, up(slots * caps, LANES)), jnp.int32),
            pltpu.SMEM((nblocks * ROWS, up(slots * caps, LANES)), jnp.int32),
            pltpu.SMEM((nblocks * slots * caps + LANES,), jnp.int32),
            pltpu.VMEM((2, npts, LANES), F32),
            pltpu.SemaphoreType.DMA(()),
        ],
        cost_estimate=pl.CostEstimate(flops=flops, bytes_accessed=1 << 22, transcendentals=0),
        compiler_params=pltpu.CompilerParams(vmem_limit_bytes=VMEM_LIMIT),
        name=name,
    )(reach, basis, factor, source, *messages, *extra)


def shards(shape_coef, cotangent, neighbours, counts, synth, weights, stiffness):
    caps, nrows, nsh = shape_coef.shape[2:]
    npoints, slots = synth.shape[0], neighbours.shape[3]
    npts = up(npoints, LANES)
    where = jnp.stack([lax.axis_index("gx"), lax.axis_index("gy")]).astype(jnp.int32)
    coef = shape_coef[0, 0].transpose(1, 0, 2).reshape(nrows * caps, nsh)
    cot = cotangent[0, 0].transpose(1, 0, 2).reshape(3 * caps, npoints)
    weight = jnp.pad(weights, (0, npts - npoints)).reshape(1, npts)

    mine = message(where, neighbours[0, 0], counts[0], coef, cot, npts)
    from_below = shifted(mine, "gy", 1)
    from_above = shifted(mine, "gy", -1)
    prepared = sources(coef, synth.T, npts, caps)
    mine, *prepared = lax.optimization_barrier((mine, *prepared))
    column = jnp.stack([from_below, mine, from_above])
    from_left = shifted(column, "gx", 1)
    from_right = shifted(column, "gx", -1)
    inner = pairs("pairs_inner", (5, 4, 3), prepared, slots, [column])
    outer = (8, 7, 6, 2, 1, 0)
    begun = (inner, weight, stiffness.reshape(1, nsh))
    grad = pairs("pairs_outer", outer, prepared, slots, [from_left, from_right], begun)
    return grad.transpose(1, 0, 2)[None, None]


def solution(mesh):
    placed = (
        P("gx", "gy", None, None, None),
        P("gx", "gy", None, None, None),
        P("gx", "gy", None, None),
        P("gx", "gy", None),
        P(),
        P(),
        P(),
    )
    return jax.shard_map(
        shards,
        mesh=mesh,
        in_specs=placed,
        out_specs=P("gx", "gy", None, None, None),
        check_vma=False,
    )
```

```python
import functools

import jax
import jax.numpy as jnp
from jax import lax
from jax.experimental import pallas as pl
from jax.experimental.pallas import tpu as pltpu
from jax.sharding import PartitionSpec as P


F32, BF16 = jnp.float32, jnp.bfloat16
DELTA_SQ = 0.0625
RADIUS_SQ_MAX = 64.0
HIGHEST = lax.Precision.HIGHEST
LANES = 128
ROWS = 8
VMEM_LIMIT = 28 << 20
TILE = 256
UNROLL = 3
VMEM = pl.BlockSpec(memory_space=pltpu.VMEM)
SMEM = pl.BlockSpec(memory_space=pltpu.SMEM)
HBM = pl.BlockSpec(memory_space=pltpu.HBM)


def up(n, m):
    return -(-n // m) * m


def shifted(block, axis, distance):
    devices = range(lax.axis_size(axis))
    route = [((i - distance) % len(devices), i) for i in devices]
    return lax.ppermute(block, axis, route)


def put(ref, value):
    for lane in range(ref.shape[0]):
        ref[lane, 0 : value.shape[0]] = value[:, lane * LANES : (lane + 1) * LANES]


def take(ref, at, stride):
    parts = [ref[lane, pl.ds(at, ROWS, stride=stride), :] for lane in range(ref.shape[0])]
    return jnp.concatenate(parts, axis=1)


def farthest(rows, caps, nblocks):
    sizes = []
    for start in range(0, rows.shape[0], rows.shape[0] // nblocks):
        x, y, z = [rows[at : at + caps] for at in range(start, start + 3 * caps, caps)]
        sizes.append(x * x + y * y + z * z)
    return jnp.max(functools.reduce(jnp.maximum, sizes))


def quotient(v, n):
    return v >> (n.bit_length() - 1) if n & (n - 1) == 0 else lax.div(v, jnp.int32(n))


def offset(block, here, width):
    step = block - here + 1
    return jnp.where(step < 0, step + width, jnp.where(step >= width, step - width, step))


def split3(v):
    high = v.astype(BF16)
    rest = v - high.astype(F32)
    mid = rest.astype(BF16)
    return high, mid, (rest - mid.astype(F32)).astype(BF16)


def cat(*xs):
    return jnp.concatenate(xs, axis=0)


def square(p):
    return p[0:1] * p[0:1] + p[1:2] * p[1:2] + p[2:3] * p[2:3]


def target_factor(p):
    row = lax.broadcasted_iota(jnp.int32, p.shape, 0)
    tail = jnp.where(row == 4, square(p) + DELTA_SQ, 0.0)
    return jnp.where(row < 3, p, jnp.where(row == 3, 1.0, tail))


def source_factor(p):
    row = lax.broadcasted_iota(jnp.int32, p.shape, 0)
    tail = jnp.where(row == 4, 1.0, 0.0)
    return jnp.where(row < 3, -2.0 * p, jnp.where(row == 3, square(p), tail))


def message_kernel(
    where_ref, near_hbm, live_hbm, coef_hbm, cot_hbm, synth_hbm,
    out_ref, basis_ref, coef_ref, near_d, live_d, cot_d, synth_d, near_v, live_v, sems, *, width_x, width_y,
):
    slots, _, caps = near_d.shape
    points, nsh = cot_d.shape[1], synth_d.shape[0]
    body = 3 * caps
    arrays = (near_hbm, near_d), (live_hbm, live_d), (coef_hbm, coef_ref), (cot_hbm, cot_d), (synth_hbm, synth_d)
    copies = [pltpu.make_async_copy(a, b, sems.at[i]) for i, (a, b) in enumerate(arrays)]
    for copy in copies:
        copy.start()
    near_v[...] = jnp.zeros_like(near_v)
    live_v[...] = jnp.zeros_like(live_v)
    out_ref[...] = jnp.zeros_like(out_ref)
    basis_ref[...] = jnp.zeros_like(basis_ref)
    copies[0].wait()
    copies[1].wait()
    for k in range(slots):
        near_v[k : k + 1, 0:caps] = near_d[k]
    live_v[0:1, 0:caps] = live_d[...]
    index = near_v[...].astype(F32).T[0:caps].astype(jnp.int32)
    target = lax.broadcasted_iota(jnp.int32, index.shape, 0)
    slot = lax.broadcasted_iota(jnp.int32, index.shape, 1)
    counts = jnp.where(target == slot, live_v[0:1], 0).astype(F32)
    counts = jnp.sum(counts, axis=1, keepdims=True)
    column = quotient(index, caps)
    line = quotient(column, width_y)
    cap = index - column * caps
    off_x = offset(line, where_ref[0], width_x)
    off_y = offset(column - line * width_y, where_ref[1], width_y)
    alive = jnp.logical_and(slot.astype(F32) < counts, slot < slots)
    group = jnp.where(alive, off_x * 3 + off_y, 9)
    marks = cat(*[jnp.where(group == g, 1.0, 0.0) for g in range(9)]).astype(BF16)
    row = lax.broadcasted_iota(jnp.int32, (LANES, LANES), 0)
    col = lax.broadcasted_iota(jnp.int32, (LANES, LANES), 1)
    before = jnp.where(row < col, 1.0, 0.0).astype(BF16)
    ranks = jnp.dot(marks, before, preferred_element_type=F32)
    sums = jnp.dot(marks, jnp.ones((LANES, LANES), BF16), preferred_element_type=F32)
    row = lax.broadcasted_iota(jnp.int32, (9 * caps, 9 * caps), 0)
    col = lax.broadcasted_iota(jnp.int32, (9 * caps, 9 * caps), 1)
    above = jnp.where(col < row, 1.0, 0.0).astype(BF16)
    starts = jnp.dot(above, sums.astype(BF16), preferred_element_type=F32)
    ranks += starts
    place = jnp.full(index.shape, -1.0, F32)
    for g in range(9):
        place = jnp.where(group == g, ranks[g * caps : (g + 1) * caps], place)
    code = (target * caps + cap).astype(F32)
    length = up(slots * caps, LANES)
    at = lax.broadcasted_iota(jnp.int32, (caps, length), 1).astype(F32)
    listed = jnp.zeros((caps, length), F32)
    for k in range(slots):
        listed += jnp.where(place[:, k : k + 1] == at, code[:, k : k + 1], 0.0)
    bounds = jnp.zeros((1, LANES), F32)
    for g in range(9):
        bounds = jnp.where(slot[0:1] == g, starts[g * caps : g * caps + 1], bounds)
    last = 9 * caps - 1
    bounds = jnp.where(slot[0:1] == 9, starts[last:] + sums[last:], bounds)

    for copy in copies[2:]:
        copy.wait()
    out_ref[0:body, 0:points] = cot_d[...]
    wide = up(points, LANES)
    out_ref[0:body, wide : wide + nsh] = coef_ref[0:body, :]
    out_ref[body : body + 1, 0:length] = jnp.sum(listed, axis=0, keepdims=True)
    out_ref[body + 1 : body + 2, 0:LANES] = bounds
    basis_ref[:, 0:points] = synth_d[...]


def message(where, near, live, coef, cot, synth_t, npts):
    slots, _, caps = near.shape
    nsh = synth_t.shape[0]
    width = npts + up(nsh, LANES)
    return pl.pallas_call(
        functools.partial(message_kernel, width_x=lax.axis_size("gx"), width_y=lax.axis_size("gy")),
        out_shape=(
            jax.ShapeDtypeStruct((3 * caps + ROWS, width), F32),
            jax.ShapeDtypeStruct((nsh, npts), F32),
            jax.ShapeDtypeStruct(coef.shape, F32),
        ),
        in_specs=[SMEM] + [HBM] * 5,
        out_specs=(VMEM,) * 3,
        scratch_shapes=[
            pltpu.VMEM(near.shape, jnp.int32),
            pltpu.VMEM(live.shape, jnp.int32),
            pltpu.VMEM(cot.shape, F32),
            pltpu.VMEM(synth_t.shape, F32),
            pltpu.VMEM((LANES, LANES), jnp.int32),
            pltpu.VMEM((ROWS, LANES), jnp.int32),
            pltpu.SemaphoreType.DMA((5,)),
        ],
        name="message",
    )(where, near, live, coef, cot, synth_t)


def sources_kernel(coef_ref, basis_ref, factor_ref, source_ref, reach_ref, points, *, caps):
    npts = basis_ref.shape[1]
    upsampled = jnp.dot(coef_ref[...], basis_ref[...], precision=HIGHEST, preferred_element_type=F32)
    points[...] = jnp.zeros_like(points)
    put(points, upsampled)
    reach_ref[0] = farthest(upsampled, caps, 1)
    pad = jnp.zeros((LANES - 6 * ROWS, npts), F32)
    for s in range(caps):
        p = take(points, s, caps)
        source_ref[s] = p
        u1, u2, u3 = [u.astype(F32) for u in split3(source_factor(p))]
        factor_ref[s] = cat(u1, u2, u1, u2, u3, u1, pad).astype(BF16)


def sources(coef, basis, caps):
    npts = basis.shape[1]
    return pl.pallas_call(
        functools.partial(sources_kernel, caps=caps),
        out_shape=(
            jax.ShapeDtypeStruct((caps, LANES, npts), BF16),
            jax.ShapeDtypeStruct((caps, ROWS, npts), F32),
            jax.ShapeDtypeStruct((1,), F32),
        ),
        in_specs=[VMEM] * 2,
        out_specs=(VMEM, VMEM, SMEM),
        scratch_shapes=[pltpu.VMEM((npts // LANES, ROWS * caps, LANES), F32)],
        compiler_params=pltpu.CompilerParams(vmem_limit_bytes=VMEM_LIMIT),
        name="sources",
    )(coef, basis)


def pairs_kernel(groups, nmsg, final, reach_ref, basis_ref, factor_ref, source_ref, *rest):
    msg_refs, rest = rest[:nmsg], rest[nmsg:]
    if final:
        begun_ref, weight_ref, stiff_ref, out_ref, *scratch = rest
    else:
        out_ref, *scratch = rest
    points, cots, base_sc, target_f, total, plan_v, plan_s, entries, column, sem = scratch
    caps, _, npts = source_ref.shape
    nsh = basis_ref.shape[0]
    nblocks, body = len(groups), 3 * caps
    tiles = [(j, min(TILE, npts - j)) for j in range(0, npts, TILE)]
    messages = [ref.at[i] for ref in msg_refs for i in range(ref.shape[0])]

    length = plan_v.shape[1]
    for b, msg in enumerate(messages):
        plan_v[b * ROWS : (b + 1) * ROWS] = msg[body : body + ROWS, 0:length].astype(jnp.int32)
    copy = pltpu.make_async_copy(plan_v, plan_s, sem)
    copy.start()
    total[...] = begun_ref[...] if final else jnp.zeros_like(total)
    flat = cat(*[msg[0:body, npts : npts + nsh] for msg in messages])
    upsampled = jnp.dot(flat, basis_ref[...], precision=HIGHEST, preferred_element_type=F32)
    put(points, upsampled)
    put(cots, cat(*[msg[0:body, 0:npts] for msg in messages]))
    for ref in (points, cots):
        ref[:, nblocks * body :] = jnp.zeros((ref.shape[0], ref.shape[1] - nblocks * body, LANES), F32)
    copy.wait()

    count = jnp.int32(0)
    for b, g in enumerate(groups):
        first, end = plan_s[b * ROWS + 1, g], plan_s[b * ROWS + 1, g + 1]

        def copy_entry(k, _):
            code = plan_s[b * ROWS, k]
            t = quotient(code, caps)
            entries[count + k - first] = ((b * body + t) << 8) + code - t * caps
            return 0

        lax.fori_loop(first, end, copy_entry, 0)
        count += end - first

    def entry(k):
        inside = k < count
        code = jnp.where(inside, entries[k], 0)
        s = code & 255
        return code >> 8, s, jnp.where(inside, s, caps)

    def squares(k, held):
        at, s, _ = entry(k)
        w1, w2, w3 = [w.astype(F32) for w in split3(target_factor(take(points, at, caps)))]
        pad = jnp.zeros((LANES - 6 * ROWS, npts), F32)
        target_f[held] = cat(w1, w1, w2, w2, w1, w3, pad).T.astype(BF16)
        for j, jc in tiles:
            base_sc[:, j : j + jc] = jnp.dot(
                target_f[held], factor_ref[s, :, j : j + jc], preferred_element_type=F32
            )
            yield

    def contract(k):
        at, s, sum_at = entry(k)
        p, c3 = take(points, at, caps), take(cots, at, caps)[0:3]
        a = cat(c3 * p[0:1], c3 * p[1:2], c3 * p[2:3], c3, jnp.zeros((4, npts), F32))
        rows = cat(*split3(a))
        for j, jc in tiles:
            r = lax.rsqrt(base_sc[:, j : j + jc])
            r3 = r * r * r
            high = r3.astype(BF16)
            low = (r3 - high.astype(F32)).astype(BF16)
            d1 = jnp.dot(rows, high, preferred_element_type=F32)
            d2 = jnp.dot(rows[0:32], low, preferred_element_type=F32)
            sums = d1[0:16] + d1[16:32] + d1[32:48] + d2[0:16] + d2[16:32]
            y = source_ref[s, :, j : j + jc]
            plain = sums[9:12]
            term = y[3:4] * (sums[0:3] - y[0:1] * plain)
            term += y[4:5] * (sums[3:6] - y[1:2] * plain)
            term += y[5:6] * (sums[6:9] - y[2:3] * plain)
            for lane in range(j // LANES, (j + jc) // LANES):
                part = term[:, lane * LANES - j : (lane + 1) * LANES - j]
                total[lane, pl.ds(pl.multiple_of(sum_at * ROWS, ROWS), 3), :] += part
            yield

    def fast_steps(q, _):
        for z in range(UNROLL):
            k = q * UNROLL + z
            now, ahead = contract(k), squares(k + 1, z % 2)
            for _ in tiles:
                next(now)
                next(ahead)
        return 0

    def exact_step(k, _):
        at, s, sum_at = entry(k)
        pad = jnp.zeros((LANES - ROWS, npts), F32)
        column[0] = cat(take(points, at, caps), pad).T
        column[1] = cat(take(cots, at, caps), pad).T
        y = source_ref[s]

        def each_chunk(i, acc):
            start = pl.multiple_of(i * LANES, LANES)
            x = column[0, pl.ds(start, LANES), :]
            numer, base = 0.0, DELTA_SQ
            for d in range(3):
                differ = x[:, d : d + 1] - y[d : d + 1]
                base = base + differ * differ
                numer = numer + differ * y[3 + d : 4 + d]
            kernel = numer / (base * jnp.sqrt(base))
            cot = column[1, pl.ds(start, LANES), :].T[0:ROWS]
            return acc + jnp.dot(cot, kernel, precision=HIGHEST, preferred_element_type=F32)

        term = lax.fori_loop(0, npts // LANES, each_chunk, jnp.zeros((ROWS, npts), F32))
        for lane in range(npts // LANES):
            part = term[0:3, lane * LANES : (lane + 1) * LANES]
            total[lane, pl.ds(pl.multiple_of(sum_at * ROWS, ROWS), 3), :] += part
        return 0

    reach = jnp.maximum(reach_ref[0], farthest(upsampled, caps, nblocks))
    expands = reach <= RADIUS_SQ_MAX

    @pl.when(jnp.logical_and(expands, count > 0))
    def _():
        for _ in squares(0, 1):
            pass
        lax.fori_loop(0, (count + UNROLL - 1) // UNROLL, fast_steps, 0)

    @pl.when(jnp.logical_not(expands))
    def _():
        lax.fori_loop(0, count, exact_step, 0)

    if not final:
        out_ref[...] = total[...]
        return
    dense = cat(*[
        jnp.concatenate([total[lane, pl.ds(d, caps, stride=ROWS), :] for lane in range(npts // LANES)], axis=1)
        for d in range(3)
    ])
    npoints = weight_ref.shape[0]
    weight = jnp.concatenate([weight_ref[...].reshape(1, npoints), jnp.zeros((1, npts - npoints), F32)], axis=1)
    scaled = dense * weight
    grad = lax.dot_general(
        scaled, basis_ref[...], (((1,), (1,)), ((), ())), precision=HIGHEST, preferred_element_type=F32
    )
    out_ref[...] = (grad * stiff_ref[...].reshape(1, nsh)).reshape(3, caps, nsh)


def pairs(name, groups, prepared, slots, messages, begun=None):
    basis, factor, source, reach = prepared
    caps, _, npts = source.shape
    nsh = basis.shape[0]
    nblocks, lanes = len(groups), npts // LANES
    final = begun is not None
    total = jax.ShapeDtypeStruct((lanes, (caps + 1) * ROWS, LANES), F32)
    out = jax.ShapeDtypeStruct((3, caps, nsh), F32) if final else total
    held = nblocks * 3 * caps + ROWS * caps
    flops = 2 * caps * nblocks * npts * npts * 64
    extra = tuple(begun) if final else ()
    return pl.pallas_call(
        functools.partial(pairs_kernel, groups, len(messages), final),
        out_shape=out,
        in_specs=[SMEM] + [VMEM] * (3 + len(messages) + len(extra)),
        out_specs=VMEM,
        scratch_shapes=[
            pltpu.VMEM((lanes, held, LANES), F32),
            pltpu.VMEM((lanes, held, LANES), F32),
            pltpu.VMEM((npts, npts), F32),
            pltpu.VMEM((2, npts, LANES), BF16),
            pltpu.VMEM(total.shape, F32),
            pltpu.VMEM((nblocks * ROWS, up(slots * caps, LANES)), jnp.int32),
            pltpu.SMEM((nblocks * ROWS, up(slots * caps, LANES)), jnp.int32),
            pltpu.SMEM((nblocks * slots * caps + LANES,), jnp.int32),
            pltpu.VMEM((2, npts, LANES), F32),
            pltpu.SemaphoreType.DMA(()),
        ],
        cost_estimate=pl.CostEstimate(flops=flops, bytes_accessed=1 << 22, transcendentals=0),
        compiler_params=pltpu.CompilerParams(vmem_limit_bytes=VMEM_LIMIT),
        name=name,
    )(reach, basis, factor, source, *messages, *extra)


def shards(shape_coef, cotangent, neighbours, counts, synth, weights, stiffness):
    caps, nrows, nsh = shape_coef.shape[2:]
    npoints, slots = synth.shape[0], neighbours.shape[3]
    npts = up(npoints, LANES)
    where = jnp.stack([lax.axis_index("gx"), lax.axis_index("gy")]).astype(jnp.int32)
    coef = shape_coef[0, 0].transpose(1, 0, 2).reshape(nrows * caps, nsh)
    cot = cotangent[0, 0].transpose(1, 0, 2).reshape(3 * caps, npoints)
    near = neighbours.transpose(0, 3, 1, 2).reshape(slots, 1, caps)

    mine, basis, coef = message(where, near, counts[0], coef, cot, synth.T, npts)
    from_below = shifted(mine, "gy", 1)
    from_above = shifted(mine, "gy", -1)
    prepared = sources(coef, basis, caps)
    mine, basis, *prepared = lax.optimization_barrier((mine, basis, *prepared))
    prepared = (basis, *prepared)
    column = jnp.stack([from_below, mine, from_above])
    from_left = shifted(column, "gx", 1)
    from_right = shifted(column, "gx", -1)
    inner = pairs("pairs_inner", (5, 4, 3), prepared, slots, [column])
    outer = (8, 7, 6, 2, 1, 0)
    begun = (inner, weights, stiffness)
    grad = pairs("pairs_outer", outer, prepared, slots, [from_left, from_right], begun)
    return grad.transpose(1, 0, 2)[None, None]


def solution(mesh):
    placed = (
        P("gx", "gy", None, None, None),
        P("gx", "gy", None, None, None),
        P("gx", "gy", None, None),
        P("gx", "gy", None),
        P(),
        P(),
        P(),
    )
    return jax.shard_map(
        shards,
        mesh=mesh,
        in_specs=placed,
        out_specs=P("gx", "gy", None, None, None),
        check_vma=False,
    )
```

```python
import functools

import jax
import jax.numpy as jnp
from jax import lax
from jax.experimental import pallas as pl
from jax.experimental.pallas import tpu as pltpu
from jax.sharding import PartitionSpec as P


F32, BF16 = jnp.float32, jnp.bfloat16
DELTA_SQ = 0.0625
RADIUS_SQ_MAX = 64.0
HIGHEST = lax.Precision.HIGHEST
LANES = 128
ROWS = 8
VMEM_LIMIT = 28 << 20
TILE = 256
UNROLL = 3
VMEM = pl.BlockSpec(memory_space=pltpu.VMEM)
SMEM = pl.BlockSpec(memory_space=pltpu.SMEM)
HBM = pl.BlockSpec(memory_space=pltpu.HBM)


def up(n, m):
    return -(-n // m) * m


def shifted(block, axis, distance):
    devices = range(lax.axis_size(axis))
    route = [((i - distance) % len(devices), i) for i in devices]
    return lax.ppermute(block, axis, route)


def put(ref, value):
    for lane in range(ref.shape[0]):
        ref[lane, 0 : value.shape[0]] = value[:, lane * LANES : (lane + 1) * LANES]


def take(ref, at, stride):
    parts = [ref[lane, pl.ds(at, ROWS, stride=stride), :] for lane in range(ref.shape[0])]
    return jnp.concatenate(parts, axis=1)


def farthest(rows, caps, nblocks):
    sizes = []
    for start in range(0, rows.shape[0], rows.shape[0] // nblocks):
        x, y, z = [rows[at : at + caps] for at in range(start, start + 3 * caps, caps)]
        sizes.append(x * x + y * y + z * z)
    return jnp.max(functools.reduce(jnp.maximum, sizes))


def quotient(v, n):
    return v >> (n.bit_length() - 1) if n & (n - 1) == 0 else lax.div(v, jnp.int32(n))


def offset(block, here, width):
    step = block - here + 1
    return jnp.where(step < 0, step + width, jnp.where(step >= width, step - width, step))


def split3(v):
    high = v.astype(BF16)
    rest = v - high.astype(F32)
    mid = rest.astype(BF16)
    return high, mid, (rest - mid.astype(F32)).astype(BF16)


def cat(*xs):
    return jnp.concatenate(xs, axis=0)


def square(p):
    return p[0:1] * p[0:1] + p[1:2] * p[1:2] + p[2:3] * p[2:3]


def target_factor(p):
    row = lax.broadcasted_iota(jnp.int32, p.shape, 0)
    tail = jnp.where(row == 4, square(p) + DELTA_SQ, 0.0)
    return jnp.where(row < 3, p, jnp.where(row == 3, 1.0, tail))


def source_factor(p):
    row = lax.broadcasted_iota(jnp.int32, p.shape, 0)
    tail = jnp.where(row == 4, 1.0, 0.0)
    return jnp.where(row < 3, -2.0 * p, jnp.where(row == 3, square(p), tail))


def message_kernel(
    near_hbm, live_hbm, coef_hbm, cot_hbm, synth_hbm,
    out_ref, basis_ref, coef_ref, near_d, live_d, cot_d, synth_d, near_v, live_v, sems, *, width_x, width_y,
):
    slots, _, caps = near_d.shape
    points, nsh = cot_d.shape[1], synth_d.shape[0]
    body = 3 * caps
    arrays = (near_hbm, near_d), (live_hbm, live_d), (coef_hbm, coef_ref), (cot_hbm, cot_d), (synth_hbm, synth_d)
    copies = [pltpu.make_async_copy(a, b, sems.at[i]) for i, (a, b) in enumerate(arrays)]
    for copy in copies:
        copy.start()
    near_v[...] = jnp.zeros_like(near_v)
    live_v[...] = jnp.zeros_like(live_v)
    out_ref[...] = jnp.zeros_like(out_ref)
    basis_ref[...] = jnp.zeros_like(basis_ref)
    copies[0].wait()
    copies[1].wait()
    for k in range(slots):
        near_v[k : k + 1, 0:caps] = near_d[k]
    live_v[0:1, 0:caps] = live_d[...]
    index = near_v[...].astype(F32).T[0:caps].astype(jnp.int32)
    target = lax.broadcasted_iota(jnp.int32, index.shape, 0)
    slot = lax.broadcasted_iota(jnp.int32, index.shape, 1)
    counts = jnp.where(target == slot, live_v[0:1], 0).astype(F32)
    counts = jnp.sum(counts, axis=1, keepdims=True)
    column = quotient(index, caps)
    line = quotient(column, width_y)
    cap = index - column * caps
    off_x = offset(line, lax.axis_index("gx"), width_x)
    off_y = offset(column - line * width_y, lax.axis_index("gy"), width_y)
    alive = jnp.logical_and(slot.astype(F32) < counts, slot < slots)
    group = jnp.where(alive, off_x * 3 + off_y, 9)
    marks = cat(*[jnp.where(group == g, 1.0, 0.0) for g in range(9)]).astype(BF16)
    row = lax.broadcasted_iota(jnp.int32, (LANES, LANES), 0)
    col = lax.broadcasted_iota(jnp.int32, (LANES, LANES), 1)
    before = jnp.where(row < col, 1.0, 0.0).astype(BF16)
    ranks = jnp.dot(marks, before, preferred_element_type=F32)
    sums = jnp.dot(marks, jnp.ones((LANES, LANES), BF16), preferred_element_type=F32)
    row = lax.broadcasted_iota(jnp.int32, (9 * caps, 9 * caps), 0)
    col = lax.broadcasted_iota(jnp.int32, (9 * caps, 9 * caps), 1)
    above = jnp.where(col < row, 1.0, 0.0).astype(BF16)
    starts = jnp.dot(above, sums.astype(BF16), preferred_element_type=F32)
    ranks += starts
    place = jnp.full(index.shape, -1.0, F32)
    for g in range(9):
        place = jnp.where(group == g, ranks[g * caps : (g + 1) * caps], place)
    code = (target * caps + cap).astype(F32)
    length = up(slots * caps, LANES)
    at = lax.broadcasted_iota(jnp.int32, (caps, length), 1).astype(F32)
    listed = jnp.zeros((caps, length), F32)
    for k in range(slots):
        listed += jnp.where(place[:, k : k + 1] == at, code[:, k : k + 1], 0.0)
    bounds = jnp.zeros((1, LANES), F32)
    for g in range(9):
        bounds = jnp.where(slot[0:1] == g, starts[g * caps : g * caps + 1], bounds)
    last = 9 * caps - 1
    bounds = jnp.where(slot[0:1] == 9, starts[last:] + sums[last:], bounds)

    for copy in copies[2:]:
        copy.wait()
    out_ref[0:body, 0:points] = cot_d[...]
    wide = up(points, LANES)
    out_ref[0:body, wide : wide + nsh] = coef_ref[0:body, :]
    out_ref[body : body + 1, 0:length] = jnp.sum(listed, axis=0, keepdims=True)
    out_ref[body + 1 : body + 2, 0:LANES] = bounds
    basis_ref[:, 0:points] = synth_d[...]


def message(near, live, coef, cot, synth_t, npts):
    slots, _, caps = near.shape
    nsh = synth_t.shape[0]
    width = npts + up(nsh, LANES)
    return pl.pallas_call(
        functools.partial(message_kernel, width_x=lax.axis_size("gx"), width_y=lax.axis_size("gy")),
        out_shape=(
            jax.ShapeDtypeStruct((3 * caps + ROWS, width), F32),
            jax.ShapeDtypeStruct((nsh, npts), F32),
            jax.ShapeDtypeStruct(coef.shape, F32),
        ),
        in_specs=[HBM] * 5,
        out_specs=(VMEM,) * 3,
        scratch_shapes=[
            pltpu.VMEM(near.shape, jnp.int32),
            pltpu.VMEM(live.shape, jnp.int32),
            pltpu.VMEM(cot.shape, F32),
            pltpu.VMEM(synth_t.shape, F32),
            pltpu.VMEM((LANES, LANES), jnp.int32),
            pltpu.VMEM((ROWS, LANES), jnp.int32),
            pltpu.SemaphoreType.DMA((5,)),
        ],
        name="message",
    )(near, live, coef, cot, synth_t)


def sources_kernel(coef_ref, basis_ref, factor_ref, source_ref, reach_ref, points, *, caps):
    npts = basis_ref.shape[1]
    upsampled = jnp.dot(coef_ref[...], basis_ref[...], precision=HIGHEST, preferred_element_type=F32)
    points[...] = jnp.zeros_like(points)
    put(points, upsampled)
    reach_ref[0] = farthest(upsampled, caps, 1)
    pad = jnp.zeros((LANES - 6 * ROWS, npts), F32)
    for s in range(caps):
        p = take(points, s, caps)
        source_ref[s] = p
        u1, u2, u3 = [u.astype(F32) for u in split3(source_factor(p))]
        factor_ref[s] = cat(u1, u2, u1, u2, u3, u1, pad).astype(BF16)


def sources(coef, basis, caps):
    npts = basis.shape[1]
    return pl.pallas_call(
        functools.partial(sources_kernel, caps=caps),
        out_shape=(
            jax.ShapeDtypeStruct((caps, LANES, npts), BF16),
            jax.ShapeDtypeStruct((caps, ROWS, npts), F32),
            jax.ShapeDtypeStruct((1,), F32),
        ),
        in_specs=[VMEM] * 2,
        out_specs=(VMEM, VMEM, SMEM),
        scratch_shapes=[pltpu.VMEM((npts // LANES, ROWS * caps, LANES), F32)],
        compiler_params=pltpu.CompilerParams(vmem_limit_bytes=VMEM_LIMIT),
        name="sources",
    )(coef, basis)


def pairs_kernel(groups, nmsg, final, reach_ref, basis_ref, factor_ref, source_ref, *rest):
    msg_refs, rest = rest[:nmsg], rest[nmsg:]
    if final:
        begun_ref, weight_ref, stiff_ref, out_ref, *scratch = rest
    else:
        out_ref, *scratch = rest
    points, cots, base_sc, target_f, total, plan_v, plan_s, entries, column, sem = scratch
    caps, _, npts = source_ref.shape
    nsh = basis_ref.shape[0]
    nblocks, body = len(groups), 3 * caps
    tiles = [(j, min(TILE, npts - j)) for j in range(0, npts, TILE)]
    messages = [ref.at[i] for ref in msg_refs for i in range(ref.shape[0])]

    length = plan_v.shape[1]
    for b, msg in enumerate(messages):
        plan_v[2 * b : 2 * b + 2] = msg[body : body + 2, 0:length].astype(jnp.int32)
    copy = pltpu.make_async_copy(plan_v, plan_s, sem)
    copy.start()
    total[...] = begun_ref[...] if final else jnp.zeros_like(total)
    flat = cat(*[msg[0:body, npts : npts + nsh] for msg in messages])
    upsampled = jnp.dot(flat, basis_ref[...], precision=HIGHEST, preferred_element_type=F32)
    put(points, upsampled)
    put(cots, cat(*[msg[0:body, 0:npts] for msg in messages]))
    for ref in (points, cots):
        ref[:, nblocks * body :] = jnp.zeros((ref.shape[0], ref.shape[1] - nblocks * body, LANES), F32)
    copy.wait()

    count = jnp.int32(0)
    for b, g in enumerate(groups):
        first, end = plan_s[2 * b + 1, g], plan_s[2 * b + 1, g + 1]

        def copy_entry(k, _):
            code = plan_s[2 * b, k]
            t = quotient(code, caps)
            entries[count + k - first] = ((b * body + t) << 8) + code - t * caps
            return 0

        lax.fori_loop(first, end, copy_entry, 0)
        count += end - first

    def entry(k):
        inside = k < count
        code = jnp.where(inside, entries[k], 0)
        s = code & 255
        return code >> 8, s, jnp.where(inside, s, caps)

    def squares(k, held):
        at, s, _ = entry(k)
        w1, w2, w3 = [w.astype(F32) for w in split3(target_factor(take(points, at, caps)))]
        pad = jnp.zeros((LANES - 6 * ROWS, npts), F32)
        target_f[held] = cat(w1, w1, w2, w2, w1, w3, pad).T.astype(BF16)
        for j, jc in tiles:
            base_sc[:, j : j + jc] = jnp.dot(
                target_f[held], factor_ref[s, :, j : j + jc], preferred_element_type=F32
            )
            yield

    def contract(k):
        at, s, sum_at = entry(k)
        p, c3 = take(points, at, caps), take(cots, at, caps)[0:3]
        a = cat(c3 * p[0:1], c3 * p[1:2], c3 * p[2:3], c3, jnp.zeros((4, npts), F32))
        rows = cat(*split3(a))
        for j, jc in tiles:
            r = lax.rsqrt(base_sc[:, j : j + jc])
            r3 = r * r * r
            high = r3.astype(BF16)
            low = (r3 - high.astype(F32)).astype(BF16)
            d1 = jnp.dot(rows, high, preferred_element_type=F32)
            d2 = jnp.dot(rows[0:32], low, preferred_element_type=F32)
            sums = d1[0:16] + d1[16:32] + d1[32:48] + d2[0:16] + d2[16:32]
            y = source_ref[s, :, j : j + jc]
            plain = sums[9:12]
            term = y[3:4] * (sums[0:3] - y[0:1] * plain)
            term += y[4:5] * (sums[3:6] - y[1:2] * plain)
            term += y[5:6] * (sums[6:9] - y[2:3] * plain)
            for lane in range(j // LANES, (j + jc) // LANES):
                part = term[:, lane * LANES - j : (lane + 1) * LANES - j]
                total[lane, pl.ds(pl.multiple_of(sum_at * ROWS, ROWS), 3), :] += part
            yield

    def fast_steps(q, _):
        for z in range(UNROLL):
            k = q * UNROLL + z
            now, ahead = contract(k), squares(k + 1, z % 2)
            for _ in tiles:
                next(now)
                next(ahead)
        return 0

    def exact_step(k, _):
        at, s, sum_at = entry(k)
        pad = jnp.zeros((LANES - ROWS, npts), F32)
        column[0] = cat(take(points, at, caps), pad).T
        column[1] = cat(take(cots, at, caps), pad).T
        y = source_ref[s]

        def each_chunk(i, acc):
            start = pl.multiple_of(i * LANES, LANES)
            x = column[0, pl.ds(start, LANES), :]
            numer, base = 0.0, DELTA_SQ
            for d in range(3):
                differ = x[:, d : d + 1] - y[d : d + 1]
                base = base + differ * differ
                numer = numer + differ * y[3 + d : 4 + d]
            kernel = numer / (base * jnp.sqrt(base))
            cot = column[1, pl.ds(start, LANES), :].T[0:ROWS]
            return acc + jnp.dot(cot, kernel, precision=HIGHEST, preferred_element_type=F32)

        term = lax.fori_loop(0, npts // LANES, each_chunk, jnp.zeros((ROWS, npts), F32))
        for lane in range(npts // LANES):
            part = term[0:3, lane * LANES : (lane + 1) * LANES]
            total[lane, pl.ds(pl.multiple_of(sum_at * ROWS, ROWS), 3), :] += part
        return 0

    reach = jnp.maximum(reach_ref[0], farthest(upsampled, caps, nblocks))
    expands = reach <= RADIUS_SQ_MAX

    @pl.when(jnp.logical_and(expands, count > 0))
    def _():
        for _ in squares(0, 1):
            pass
        lax.fori_loop(0, (count + UNROLL - 1) // UNROLL, fast_steps, 0)

    @pl.when(jnp.logical_not(expands))
    def _():
        lax.fori_loop(0, count, exact_step, 0)

    if not final:
        out_ref[...] = total[...]
        return
    dense = cat(*[
        jnp.concatenate([total[lane, pl.ds(d, caps, stride=ROWS), :] for lane in range(npts // LANES)], axis=1)
        for d in range(3)
    ])
    npoints = weight_ref.shape[0]
    weight = jnp.concatenate([weight_ref[...].reshape(1, npoints), jnp.zeros((1, npts - npoints), F32)], axis=1)
    scaled = dense * weight
    grad = lax.dot_general(
        scaled, basis_ref[...], (((1,), (1,)), ((), ())), precision=HIGHEST, preferred_element_type=F32
    )
    out_ref[...] = (grad * stiff_ref[...].reshape(1, nsh)).reshape(3, caps, nsh)


def pairs(name, groups, prepared, slots, messages, begun=None):
    basis, factor, source, reach = prepared
    caps, _, npts = source.shape
    nsh = basis.shape[0]
    nblocks, lanes = len(groups), npts // LANES
    final = begun is not None
    total = jax.ShapeDtypeStruct((lanes, (caps + 1) * ROWS, LANES), F32)
    out = jax.ShapeDtypeStruct((3, caps, nsh), F32) if final else total
    held = nblocks * 3 * caps + ROWS * caps
    flops = 2 * caps * nblocks * npts * npts * 64
    extra = tuple(begun) if final else ()
    return pl.pallas_call(
        functools.partial(pairs_kernel, groups, len(messages), final),
        out_shape=out,
        in_specs=[SMEM] + [VMEM] * (3 + len(messages) + len(extra)),
        out_specs=VMEM,
        scratch_shapes=[
            pltpu.VMEM((lanes, held, LANES), F32),
            pltpu.VMEM((lanes, held, LANES), F32),
            pltpu.VMEM((npts, npts), F32),
            pltpu.VMEM((2, npts, LANES), BF16),
            pltpu.VMEM(total.shape, F32),
            pltpu.VMEM((up(2 * nblocks, ROWS), up(slots * caps, LANES)), jnp.int32),
            pltpu.SMEM((up(2 * nblocks, ROWS), up(slots * caps, LANES)), jnp.int32),
            pltpu.SMEM((nblocks * slots * caps + LANES,), jnp.int32),
            pltpu.VMEM((2, npts, LANES), F32),
            pltpu.SemaphoreType.DMA(()),
        ],
        cost_estimate=pl.CostEstimate(flops=flops, bytes_accessed=1 << 22, transcendentals=0),
        compiler_params=pltpu.CompilerParams(vmem_limit_bytes=VMEM_LIMIT),
        name=name,
    )(reach, basis, factor, source, *messages, *extra)


def shards(shape_coef, cotangent, neighbours, counts, synth, weights, stiffness):
    caps, nrows, nsh = shape_coef.shape[2:]
    npoints, slots = synth.shape[0], neighbours.shape[3]
    npts = up(npoints, LANES)
    coef = shape_coef[0, 0].transpose(1, 0, 2).reshape(nrows * caps, nsh)
    cot = cotangent[0, 0].transpose(1, 0, 2).reshape(3 * caps, npoints)
    near = neighbours.transpose(0, 3, 1, 2).reshape(slots, 1, caps)

    mine, basis, coef = message(near, counts[0], coef, cot, synth.T, npts)
    from_below = shifted(mine, "gy", 1)
    from_above = shifted(mine, "gy", -1)
    prepared = sources(coef, basis, caps)
    mine, basis, *prepared = lax.optimization_barrier((mine, basis, *prepared))
    prepared = (basis, *prepared)
    column = jnp.stack([from_below, mine, from_above])
    from_left = shifted(column, "gx", 1)
    from_right = shifted(column, "gx", -1)
    inner = pairs("pairs_inner", (5, 4, 3), prepared, slots, [column])
    outer = (8, 7, 6, 2, 1, 0)
    begun = (inner, weights, stiffness)
    grad = pairs("pairs_outer", outer, prepared, slots, [from_left, from_right], begun)
    return grad.transpose(1, 0, 2)[None, None]


def solution(mesh):
    placed = (
        P("gx", "gy", None, None, None),
        P("gx", "gy", None, None, None),
        P("gx", "gy", None, None),
        P("gx", "gy", None),
        P(),
        P(),
        P(),
    )
    return jax.shard_map(
        shards,
        mesh=mesh,
        in_specs=placed,
        out_specs=P("gx", "gy", None, None, None),
        check_vma=False,
    )
```

```python
import functools

import jax
import jax.numpy as jnp
from jax import lax
from jax.experimental import pallas as pl
from jax.experimental.pallas import tpu as pltpu
from jax.sharding import PartitionSpec as P


F32, BF16 = jnp.float32, jnp.bfloat16
DELTA_SQ = 0.0625
RADIUS_SQ_MAX = 64.0
HIGHEST = lax.Precision.HIGHEST
LANES = 128
ROWS = 8
VMEM_LIMIT = 28 << 20
TILE = 256
UNROLL = 3
VMEM = pl.BlockSpec(memory_space=pltpu.VMEM)
SMEM = pl.BlockSpec(memory_space=pltpu.SMEM)
HBM = pl.BlockSpec(memory_space=pltpu.HBM)


def up(n, m):
    return -(-n // m) * m


def shifted(block, axis, distance):
    devices = range(lax.axis_size(axis))
    route = [((i - distance) % len(devices), i) for i in devices]
    return lax.ppermute(block, axis, route)


def put(ref, value):
    for lane in range(ref.shape[0]):
        ref[lane, 0 : value.shape[0]] = value[:, lane * LANES : (lane + 1) * LANES]


def take(ref, at, stride):
    parts = [ref[lane, pl.ds(at, ROWS, stride=stride), :] for lane in range(ref.shape[0])]
    return jnp.concatenate(parts, axis=1)


def farthest(rows, caps, nblocks):
    sizes = []
    for start in range(0, rows.shape[0], rows.shape[0] // nblocks):
        x, y, z = [rows[at : at + caps] for at in range(start, start + 3 * caps, caps)]
        sizes.append(x * x + y * y + z * z)
    return jnp.max(functools.reduce(jnp.maximum, sizes))


def quotient(v, n):
    return v >> (n.bit_length() - 1) if n & (n - 1) == 0 else lax.div(v, jnp.int32(n))


def offset(block, here, width):
    step = block - here + 1
    return jnp.where(step < 0, step + width, jnp.where(step >= width, step - width, step))


def split3(v):
    high = v.astype(BF16)
    rest = v - high.astype(F32)
    mid = rest.astype(BF16)
    return high, mid, (rest - mid.astype(F32)).astype(BF16)


def cat(*xs):
    return jnp.concatenate(xs, axis=0)


def square(p):
    return p[0:1] * p[0:1] + p[1:2] * p[1:2] + p[2:3] * p[2:3]


def target_factor(p):
    row = lax.broadcasted_iota(jnp.int32, p.shape, 0)
    tail = jnp.where(row == 4, square(p) + DELTA_SQ, 0.0)
    return jnp.where(row < 3, p, jnp.where(row == 3, 1.0, tail))


def source_factor(p):
    row = lax.broadcasted_iota(jnp.int32, p.shape, 0)
    tail = jnp.where(row == 4, 1.0, 0.0)
    return jnp.where(row < 3, -2.0 * p, jnp.where(row == 3, square(p), tail))


def message_kernel(
    near_hbm, live_hbm, coef_hbm, cot_hbm, synth_hbm,
    out_ref, basis_ref, coef_ref, near_d, live_d, cot_d, synth_d, near_v, live_v, sems, *, width_x, width_y,
):
    slots, _, caps = near_d.shape
    points, nsh = cot_d.shape[1], synth_d.shape[0]
    body = 3 * caps
    arrays = (near_hbm, near_d), (live_hbm, live_d), (coef_hbm, coef_ref), (cot_hbm, cot_d), (synth_hbm, synth_d)
    copies = [pltpu.make_async_copy(a, b, sems.at[i]) for i, (a, b) in enumerate(arrays)]
    for copy in copies:
        copy.start()
    near_v[...] = jnp.zeros_like(near_v)
    live_v[...] = jnp.zeros_like(live_v)
    out_ref[...] = jnp.zeros_like(out_ref)
    basis_ref[...] = jnp.zeros_like(basis_ref)
    copies[0].wait()
    copies[1].wait()
    for k in range(slots):
        near_v[k : k + 1, 0:caps] = near_d[k]
    live_v[0:1, 0:caps] = live_d[...]
    index = near_v[...].astype(F32).T[0:caps].astype(jnp.int32)
    target = lax.broadcasted_iota(jnp.int32, index.shape, 0)
    slot = lax.broadcasted_iota(jnp.int32, index.shape, 1)
    counts = jnp.where(target == slot, live_v[0:1], 0).astype(F32)
    counts = jnp.sum(counts, axis=1, keepdims=True)
    column = quotient(index, caps)
    line = quotient(column, width_y)
    cap = index - column * caps
    off_x = offset(line, lax.axis_index("gx"), width_x)
    off_y = offset(column - line * width_y, lax.axis_index("gy"), width_y)
    alive = jnp.logical_and(slot.astype(F32) < counts, slot < slots)
    group = jnp.where(alive, off_x * 3 + off_y, 9)
    marks = cat(*[jnp.where(group == g, 1.0, 0.0) for g in range(9)]).astype(BF16)
    row = lax.broadcasted_iota(jnp.int32, (LANES, LANES), 0)
    col = lax.broadcasted_iota(jnp.int32, (LANES, LANES), 1)
    before = jnp.where(row < col, 1.0, 0.0).astype(BF16)
    ranks = jnp.dot(marks, before, preferred_element_type=F32)
    sums = jnp.dot(marks, jnp.ones((LANES, LANES), BF16), preferred_element_type=F32)
    row = lax.broadcasted_iota(jnp.int32, (9 * caps, 9 * caps), 0)
    col = lax.broadcasted_iota(jnp.int32, (9 * caps, 9 * caps), 1)
    above = jnp.where(col < row, 1.0, 0.0).astype(BF16)
    starts = jnp.dot(above, sums.astype(BF16), preferred_element_type=F32)
    ranks += starts
    place = jnp.full(index.shape, -1.0, F32)
    for g in range(9):
        place = jnp.where(group == g, ranks[g * caps : (g + 1) * caps], place)
    code = (target * caps + cap).astype(F32)
    length = up(slots * caps, LANES)
    at = lax.broadcasted_iota(jnp.int32, (caps, length), 1).astype(F32)
    listed = jnp.zeros((caps, length), F32)
    for k in range(slots):
        listed += jnp.where(place[:, k : k + 1] == at, code[:, k : k + 1], 0.0)
    bounds = jnp.zeros((1, LANES), F32)
    for g in range(9):
        bounds = jnp.where(slot[0:1] == g, starts[g * caps : g * caps + 1], bounds)
    last = 9 * caps - 1
    bounds = jnp.where(slot[0:1] == 9, starts[last:] + sums[last:], bounds)

    for copy in copies[2:]:
        copy.wait()
    out_ref[0:body, 0:points] = cot_d[...]
    wide = up(points, LANES)
    out_ref[0:body, wide : wide + nsh] = coef_ref[0:body, :]
    out_ref[body : body + 1, 0:length] = jnp.sum(listed, axis=0, keepdims=True)
    out_ref[body + 1 : body + 2, 0:LANES] = bounds
    basis_ref[:, 0:points] = synth_d[...]


def message(near, live, coef, cot, synth_t, npts):
    slots, _, caps = near.shape
    nsh = synth_t.shape[0]
    width = npts + up(nsh, LANES)
    return pl.pallas_call(
        functools.partial(message_kernel, width_x=lax.axis_size("gx"), width_y=lax.axis_size("gy")),
        out_shape=(
            jax.ShapeDtypeStruct((3 * caps + ROWS, width), F32),
            jax.ShapeDtypeStruct((nsh, npts), F32),
            jax.ShapeDtypeStruct(coef.shape, F32),
        ),
        in_specs=[HBM] * 5,
        out_specs=(VMEM,) * 3,
        scratch_shapes=[
            pltpu.VMEM(near.shape, jnp.int32),
            pltpu.VMEM(live.shape, jnp.int32),
            pltpu.VMEM(cot.shape, F32),
            pltpu.VMEM(synth_t.shape, F32),
            pltpu.VMEM((LANES, LANES), jnp.int32),
            pltpu.VMEM((ROWS, LANES), jnp.int32),
            pltpu.SemaphoreType.DMA((5,)),
        ],
        name="message",
    )(near, live, coef, cot, synth_t)


def sources_kernel(coef_ref, basis_ref, factor_ref, source_ref, reach_ref, points, *, caps):
    npts = basis_ref.shape[1]
    upsampled = jnp.dot(coef_ref[...], basis_ref[...], precision=HIGHEST, preferred_element_type=F32)
    points[...] = jnp.zeros_like(points)
    put(points, upsampled)
    reach_ref[0] = farthest(upsampled, caps, 1)
    pad = jnp.zeros((LANES - 6 * ROWS, npts), F32)
    for s in range(caps):
        p = take(points, s, caps)
        source_ref[s] = p
        u1, u2, u3 = [u.astype(F32) for u in split3(source_factor(p))]
        factor_ref[s] = cat(u1, u2, u1, u2, u3, u1, pad).astype(BF16)


def sources(coef, basis, caps):
    npts = basis.shape[1]
    return pl.pallas_call(
        functools.partial(sources_kernel, caps=caps),
        out_shape=(
            jax.ShapeDtypeStruct((caps, LANES, npts), BF16),
            jax.ShapeDtypeStruct((caps, ROWS, npts), F32),
            jax.ShapeDtypeStruct((1,), F32),
        ),
        in_specs=[VMEM] * 2,
        out_specs=(VMEM, VMEM, SMEM),
        scratch_shapes=[pltpu.VMEM((npts // LANES, ROWS * caps, LANES), F32)],
        compiler_params=pltpu.CompilerParams(vmem_limit_bytes=VMEM_LIMIT),
        name="sources",
    )(coef, basis)


def pairs_kernel(groups, nmsg, final, reach_ref, basis_ref, factor_ref, source_ref, *rest):
    msg_refs, rest = rest[:nmsg], rest[nmsg:]
    if final:
        begun_ref, weight_ref, stiff_ref, out_ref, *scratch = rest
    else:
        out_ref, *scratch = rest
    points, cots, base_sc, target_f, total, plan_v, plan_s, entries, column, sem = scratch
    caps, _, npts = source_ref.shape
    nsh = basis_ref.shape[0]
    nblocks, body = len(groups), 3 * caps
    tiles = [(j, min(TILE, npts - j)) for j in range(0, npts, TILE)]
    messages = [ref.at[i] for ref in msg_refs for i in range(ref.shape[0])]

    length = plan_v.shape[1]
    for b, msg in enumerate(messages):
        plan_v[2 * b : 2 * b + 2] = msg[body : body + 2, 0:length].astype(jnp.int32)
    copy = pltpu.make_async_copy(plan_v, plan_s, sem)
    copy.start()
    total[...] = begun_ref[...] if final else jnp.zeros_like(total)
    flat = cat(*[msg[0:body, npts : npts + nsh] for msg in messages])
    upsampled = jnp.dot(flat, basis_ref[...], precision=HIGHEST, preferred_element_type=F32)
    put(points, upsampled)
    put(cots, cat(*[msg[0:body, 0:npts] for msg in messages]))
    for ref in (points, cots):
        ref[:, nblocks * body :] = jnp.zeros((ref.shape[0], ref.shape[1] - nblocks * body, LANES), F32)
    copy.wait()

    count = jnp.int32(0)
    for b, g in enumerate(groups):
        first, end = plan_s[2 * b + 1, g], plan_s[2 * b + 1, g + 1]

        def copy_entry(k, _):
            code = plan_s[2 * b, k]
            t = quotient(code, caps)
            entries[count + k - first] = ((b * body + t) << 8) + code - t * caps
            return 0

        lax.fori_loop(first, end, copy_entry, 0)
        count += end - first

    def entry(k):
        inside = k < count
        code = jnp.where(inside, entries[k], 0)
        s = code & 255
        return code >> 8, s, jnp.where(inside, s, caps)

    def squares(k, held):
        at, s, _ = entry(k)
        w1, w2, w3 = [w.astype(F32) for w in split3(target_factor(take(points, at, caps)))]
        pad = jnp.zeros((LANES - 6 * ROWS, npts), F32)
        target_f[held] = cat(w1, w1, w2, w2, w1, w3, pad).T.astype(BF16)
        for j, jc in tiles:
            base_sc[:, j : j + jc] = jnp.dot(
                target_f[held], factor_ref[s, :, j : j + jc], preferred_element_type=F32
            )
            yield

    def contract(k):
        at, s, sum_at = entry(k)
        p, c3 = take(points, at, caps), take(cots, at, caps)[0:3]
        a = cat(c3 * p[0:1], c3 * p[1:2], c3 * p[2:3], c3, jnp.zeros((4, npts), F32))
        rows = cat(*split3(a))
        for j, jc in tiles:
            r = lax.rsqrt(base_sc[:, j : j + jc])
            r3 = r * r * r
            high = r3.astype(BF16)
            low = (r3 - high.astype(F32)).astype(BF16)
            d1 = jnp.dot(rows, high, preferred_element_type=F32)
            d2 = jnp.dot(rows[0:32], low, preferred_element_type=F32)
            sums = d1[0:16] + d1[16:32] + d1[32:48] + d2[0:16] + d2[16:32]
            y = source_ref[s, :, j : j + jc]
            plain = sums[9:12]
            term = y[3:4] * (sums[0:3] - y[0:1] * plain)
            term += y[4:5] * (sums[3:6] - y[1:2] * plain)
            term += y[5:6] * (sums[6:9] - y[2:3] * plain)
            for lane in range(j // LANES, (j + jc) // LANES):
                part = term[:, lane * LANES - j : (lane + 1) * LANES - j]
                total[lane, pl.ds(pl.multiple_of(sum_at * ROWS, ROWS), 3), :] += part
            yield

    def fast_steps(unroll, first, q, _):
        for z in range(unroll):
            k = first + q * unroll + z
            now, ahead = contract(k), squares(k + 1, z % 2)
            for _ in tiles:
                next(now)
                next(ahead)
        return 0

    def exact_step(k, _):
        at, s, sum_at = entry(k)
        pad = jnp.zeros((LANES - ROWS, npts), F32)
        column[0] = cat(take(points, at, caps), pad).T
        column[1] = cat(take(cots, at, caps), pad).T
        y = source_ref[s]

        def each_chunk(i, acc):
            start = pl.multiple_of(i * LANES, LANES)
            x = column[0, pl.ds(start, LANES), :]
            numer, base = 0.0, DELTA_SQ
            for d in range(3):
                differ = x[:, d : d + 1] - y[d : d + 1]
                base = base + differ * differ
                numer = numer + differ * y[3 + d : 4 + d]
            kernel = numer / (base * jnp.sqrt(base))
            cot = column[1, pl.ds(start, LANES), :].T[0:ROWS]
            return acc + jnp.dot(cot, kernel, precision=HIGHEST, preferred_element_type=F32)

        term = lax.fori_loop(0, npts // LANES, each_chunk, jnp.zeros((ROWS, npts), F32))
        for lane in range(npts // LANES):
            part = term[0:3, lane * LANES : (lane + 1) * LANES]
            total[lane, pl.ds(pl.multiple_of(sum_at * ROWS, ROWS), 3), :] += part
        return 0

    reach = jnp.maximum(reach_ref[0], farthest(upsampled, caps, nblocks))
    expands = reach <= RADIUS_SQ_MAX

    @pl.when(jnp.logical_and(expands, count > 0))
    def _():
        for _ in squares(0, 1):
            pass
        whole = lax.div(count, jnp.int32(UNROLL))
        lax.fori_loop(0, whole, functools.partial(fast_steps, UNROLL, 0), 0)
        first = whole * UNROLL
        lax.fori_loop(0, count - first, functools.partial(fast_steps, 1, first), 0)

    @pl.when(jnp.logical_not(expands))
    def _():
        lax.fori_loop(0, count, exact_step, 0)

    if not final:
        out_ref[...] = total[...]
        return
    dense = cat(*[
        jnp.concatenate([total[lane, pl.ds(d, caps, stride=ROWS), :] for lane in range(npts // LANES)], axis=1)
        for d in range(3)
    ])
    npoints = weight_ref.shape[0]
    weight = jnp.concatenate([weight_ref[...].reshape(1, npoints), jnp.zeros((1, npts - npoints), F32)], axis=1)
    scaled = dense * weight
    grad = lax.dot_general(
        scaled, basis_ref[...], (((1,), (1,)), ((), ())), precision=HIGHEST, preferred_element_type=F32
    )
    out_ref[...] = (grad * stiff_ref[...].reshape(1, nsh)).reshape(3, caps, nsh)


def pairs(name, groups, prepared, slots, messages, begun=None):
    basis, factor, source, reach = prepared
    caps, _, npts = source.shape
    nsh = basis.shape[0]
    nblocks, lanes = len(groups), npts // LANES
    final = begun is not None
    total = jax.ShapeDtypeStruct((lanes, (caps + 1) * ROWS, LANES), F32)
    out = jax.ShapeDtypeStruct((3, caps, nsh), F32) if final else total
    held = nblocks * 3 * caps + ROWS * caps
    flops = 2 * caps * nblocks * npts * npts * 64
    extra = tuple(begun) if final else ()
    return pl.pallas_call(
        functools.partial(pairs_kernel, groups, len(messages), final),
        out_shape=out,
        in_specs=[SMEM] + [VMEM] * (3 + len(messages) + len(extra)),
        out_specs=VMEM,
        scratch_shapes=[
            pltpu.VMEM((lanes, held, LANES), F32),
            pltpu.VMEM((lanes, held, LANES), F32),
            pltpu.VMEM((npts, npts), F32),
            pltpu.VMEM((2, npts, LANES), BF16),
            pltpu.VMEM(total.shape, F32),
            pltpu.VMEM((up(2 * nblocks, ROWS), up(slots * caps, LANES)), jnp.int32),
            pltpu.SMEM((up(2 * nblocks, ROWS), up(slots * caps, LANES)), jnp.int32),
            pltpu.SMEM((nblocks * slots * caps + LANES,), jnp.int32),
            pltpu.VMEM((2, npts, LANES), F32),
            pltpu.SemaphoreType.DMA(()),
        ],
        cost_estimate=pl.CostEstimate(flops=flops, bytes_accessed=1 << 22, transcendentals=0),
        compiler_params=pltpu.CompilerParams(vmem_limit_bytes=VMEM_LIMIT),
        name=name,
    )(reach, basis, factor, source, *messages, *extra)


def shards(shape_coef, cotangent, neighbours, counts, synth, weights, stiffness):
    caps, nrows, nsh = shape_coef.shape[2:]
    npoints, slots = synth.shape[0], neighbours.shape[3]
    npts = up(npoints, LANES)
    coef = shape_coef[0, 0].transpose(1, 0, 2).reshape(nrows * caps, nsh)
    cot = cotangent[0, 0].transpose(1, 0, 2).reshape(3 * caps, npoints)
    near = neighbours.transpose(0, 3, 1, 2).reshape(slots, 1, caps)

    mine, basis, coef = message(near, counts[0], coef, cot, synth.T, npts)
    from_below = shifted(mine, "gy", 1)
    from_above = shifted(mine, "gy", -1)
    prepared = sources(coef, basis, caps)
    mine, basis, *prepared = lax.optimization_barrier((mine, basis, *prepared))
    prepared = (basis, *prepared)
    column = jnp.stack([from_below, mine, from_above])
    from_left = shifted(column, "gx", 1)
    from_right = shifted(column, "gx", -1)
    inner = pairs("pairs_inner", (5, 4, 3), prepared, slots, [column])
    outer = (8, 7, 6, 2, 1, 0)
    begun = (inner, weights, stiffness)
    grad = pairs("pairs_outer", outer, prepared, slots, [from_left, from_right], begun)
    return grad.transpose(1, 0, 2)[None, None]


def solution(mesh):
    placed = (
        P("gx", "gy", None, None, None),
        P("gx", "gy", None, None, None),
        P("gx", "gy", None, None),
        P("gx", "gy", None),
        P(),
        P(),
        P(),
    )
    return jax.shard_map(
        shards,
        mesh=mesh,
        in_specs=placed,
        out_specs=P("gx", "gy", None, None, None),
        check_vma=False,
    )
```
